32 devices in a mesh: tile: 8 (over z, y), view: 4 (over x, core).
Axes of the slice: x: 2, y: 2, z: 4, core: 2. Of those that a mesh axis runs over, the one named last changes fastest.
Arguments:
- recorded: bfloat16 [4, 128, 256, 256], P('view', 'tile'), may hold values from 0.099609375 to 10
- estimate: float32 [128, 256, 256], P('tile', 'view'), may hold values from 0.5 to 2
- psf_taps: float32 [16, 3, 31], replicated, may hold values from 0.05 to 1
- half_width: int32 [16, 3], replicated, may hold values from 8 to 15
- assign: int32 [4], replicated, may hold values from 0 to 15
- flags: int32 [16, 32], P('tile', 'view'), may hold values 0 or 1
Outputs:
- restored: float32 [128, 256, 256], P('tile', 'view')
The draws below stay inside these ranges and needn't reach their ends.
All inputs are finite; a program needn't handle non-finite values. No bound on the sum of `flags` on one device may be relied on, other than what follows from the above.
Results may differ from the reference program's by a relative error of at most 0.0007.
Values may be sent and summed in bfloat16 or wider, within the bound.
A program may use at most 64 MiB of HBM per device.

```python
import math
import jax
import jax.numpy as jnp
from jax import lax

NY = 256
NZ = 256
VIEWS = 4
KERNELS = 16
TAPS = 31
ITERS = 1
NX = 128


def plant(entries, rng, least, top_value):
    extent = entries.shape
    spot = [jax.random.randint(jax.random.fold_in(rng, axis), (), 0, extent[axis]) for axis in range(len(extent))]
    entries = entries.at[tuple(spot)].set(least)
    longest = extent.index(max(extent))
    spot[longest] = (spot[longest] + 1) % extent[longest]
    return entries.at[tuple(spot)].set(top_value)


def block_scale(stream_key, shape, shards, low, top_value):
    level, own = 1.0, jax.random.fold_in(stream_key, 6)
    for axis_at, shards_of in shards:
        steps = jnp.exp(jax.random.uniform(jax.random.fold_in(own, axis_at), (shards_of,), jnp.float32, low / len(shards), top_value / len(shards)))
        level = level * jnp.repeat(steps, shape[axis_at] // shards_of).reshape([-1 if axis == axis_at else 1 for axis in range(len(shape))])
    return level


def setup_inputs(seed: int = 0) -> dict:
    splits = jax.random.split(jax.random.key(seed), 7)
    return {
        "recorded": jnp.clip(jnp.exp(math.log(10.0) - 4.609084 * jax.random.uniform(splits[0], (VIEWS, NX, NY, NZ), jnp.float32) ** block_scale(splits[0], (VIEWS, NX, NY, NZ), ((0, 4), (1, 8)), -0.2, 0.2)), 0.099609375, 10.0).astype(jnp.bfloat16),
        "estimate": jnp.clip(jnp.exp(math.log(2.0) - 1.3862944 * jax.random.uniform(splits[1], (NX, NY, NZ), jnp.float32) ** block_scale(splits[1], (NX, NY, NZ), ((0, 8), (1, 4)), -0.2, 0.2)), 0.5, 2.0),
        "psf_taps": jnp.clip(jnp.exp(jax.random.uniform(splits[2], (KERNELS, 3, TAPS), jnp.float32, math.log(0.05), math.log(1.0))), 0.05, 1.0),
        "half_width": plant(jax.random.randint(splits[3], (KERNELS, 3), 8, 16), jax.random.fold_in(splits[3], 1), 8, 15).astype(jnp.int32),
        "assign": plant(jax.random.randint(splits[4], (VIEWS,), 0, KERNELS), jax.random.fold_in(splits[4], 1), 0, KERNELS - 1).astype(jnp.int32),
        "flags": plant((jax.random.randint(splits[5], (NX // 8, NY // 8), 0, 4) < 3).astype(jnp.int32), jax.random.fold_in(splits[5], 1), 0, 1),
    }


def make_kernels(psf_taps, half_width, assign):
    offsets = jnp.abs(jnp.arange(TAPS) - TAPS // 2)
    keep = (offsets[None, None, :] <= half_width[:, :, None]).astype(jnp.float32)
    raw = psf_taps * keep
    kern = raw / jnp.sum(raw, axis=-1, keepdims=True)
    picker = (assign[:, None] == jnp.arange(KERNELS)[None, :]).astype(jnp.float32)
    return jnp.einsum("sv,vaj->saj", picker, kern, precision=lax.Precision.HIGHEST)


def band_matrix(kernel, length):
    rows = jnp.arange(length)[:, None]
    cols = jnp.arange(length)[None, :]
    offset = rows - cols + TAPS // 2
    hits = (offset[None, :, :] == jnp.arange(TAPS)[:, None, None]).astype(jnp.float32)
    return jnp.sum(kernel[:, None, None] * hits, axis=0)


def blur_three(volume, kernels):
    padded = jnp.pad(volume, ((TAPS // 2, TAPS // 2), (0, 0), (0, 0)))
    length = volume.shape[0]
    along = jnp.zeros_like(volume)
    for j in range(TAPS):
        along = along + kernels[0, j] * padded[j:j + length]
    along = jnp.einsum("xpz,pi->xiz", along, band_matrix(kernels[1], volume.shape[1]), precision=lax.Precision.HIGHEST)
    return jnp.einsum("xyp,pi->xyi", along, band_matrix(kernels[2], volume.shape[2]), precision=lax.Precision.HIGHEST)


def reference(recorded, estimate, psf_taps, half_width, assign, flags):
    kernels = make_kernels(psf_taps, half_width, assign)
    flipped = kernels[:, :, ::-1]
    cells = jnp.repeat(jnp.repeat(flags, 8, axis=0), 8, axis=1)[:, :, None] > 0
    current = estimate
    for step in range(ITERS):
        rounded = lax.optimization_barrier(current.astype(jnp.bfloat16)).astype(jnp.float32)

        def one_slot(total, items):
            slot_data, slot_kern, slot_flip = items
            blurred = blur_three(rounded, slot_kern)
            ratio = (slot_data.astype(jnp.float32) / blurred).astype(jnp.bfloat16)
            ratio = lax.optimization_barrier(ratio).astype(jnp.float32)
            return total + blur_three(ratio, slot_flip), None

        total, _ = lax.scan(one_slot, jnp.zeros_like(current), (recorded, kernels, flipped))
        correction = total / VIEWS
        current = jnp.where(cells, current * correction, current)
    return current
```

```python
import jax
import jax.numpy as jnp
from jax import lax
from jax.experimental import pallas as pl
from jax.experimental.pallas import tpu as pltpu
from jax.sharding import PartitionSpec as P

TAPS = 31
HALF = TAPS // 2
GROUP = 8
CHUNK = 16
STACK = 4
F32 = jnp.float32
BF16 = jnp.bfloat16
MESH = pl.DeviceIdType.MESH


def dot(a, b):
    return jnp.dot(a, b, preferred_element_type=F32)


def picked_taps(entry, half_ref, psf_ref, taps):
    for d in range(3):
        taps[d:d + 1, 0:TAPS] = psf_ref[d, pl.ds(entry, 1), :]
    row = lax.broadcasted_iota(jnp.int32, taps.shape, 0)
    col = lax.broadcasted_iota(jnp.int32, taps.shape, 1)
    width = jnp.where(
        row == 0, half_ref[0, entry], jnp.where(row == 1, half_ref[1, entry], half_ref[2, entry])
    )
    keep = (jnp.abs(col - HALF) <= width) & (col < TAPS) & (row < 3)
    return jnp.where(keep, taps[...], 0.0).astype(BF16).astype(F32)


def band(line, size):
    rolled = pltpu.roll(
        jnp.broadcast_to(line, (size, size)), size - HALF, 1, stride=1, stride_axis=0
    )
    row = lax.broadcasted_iota(jnp.int32, (size, size), 0)
    col = lax.broadcasted_iota(jnp.int32, (size, size), 1)
    return jnp.where(jnp.abs(row - col) <= HALF, rolled, 0.0)


def stacked_band(line):
    width = line.shape[1]
    blocks = [
        pltpu.roll(
            jnp.broadcast_to(line, (CHUNK, width)), 3 * CHUNK * i + CHUNK - HALF, 1,
            stride=1, stride_axis=0,
        )
        for i in range(STACK)
    ]
    return jnp.concatenate(blocks, axis=0)[:, :3 * CHUNK * STACK].astype(BF16)


def kernel(
    assign_ref, half_ref, psf_ref, estimate, recorded_hbm, out,
    rounded, taps, scales, wide_a, wide_b, cy, cyt, cz, czt, recorded,
    from_low, from_high, mixed, ratios,
    to_low, to_high, back_low, back_high,
    own_sem, rec_send, rec_recv, halo_send, halo_recv,
    mix_send, mix_recv, ratio_send, ratio_recv, sum_send, sum_recv,
):
    slab, quarter, depth = rounded.shape
    views = recorded.shape[0]
    chunks = quarter // CHUNK
    tile, view = lax.axis_index("tile"), lax.axis_index("view")
    last = lax.axis_size("tile") - 1
    has_low, has_high = tile > 0, tile < last
    odd = lax.rem(view, 2)
    inner = view + 1 - 2 * odd
    outer = view - 1 + 2 * odd
    has_outer = (outer >= 0) & (outer < views)

    def place(c, parity):
        return c + parity * (chunks - 1 - 2 * c)

    def ys(c, base=0, size=CHUNK):
        return pl.ds(pl.multiple_of(base + place(c, odd) * CHUNK, CHUNK), size)

    def peer(k):
        return lax.rem(view + k, views)

    def remote(src, dst, send, recv, device):
        return pltpu.make_async_remote_copy(
            src_ref=src, dst_ref=dst, send_sem=send, recv_sem=recv,
            device_id=device, device_id_type=MESH,
        )

    def halo_up(c):
        return remote(
            rounded.at[slab - HALF:slab, ys(c)], from_low.at[slab - HALF:slab, ys(c)],
            halo_send.at[0, c], halo_recv.at[0, c], {"tile": tile + 1},
        )

    def halo_down(c):
        return remote(
            rounded.at[0:HALF, ys(c)], from_high.at[0:HALF, ys(c)],
            halo_send.at[1, c], halo_recv.at[1, c], {"tile": tile - 1},
        )

    def sum_up(c):
        return remote(
            to_high.at[:, ys(c)], back_low.at[:, ys(c)],
            sum_send.at[0, c], sum_recv.at[0, c], {"tile": tile + 1},
        )

    def sum_down(c):
        return remote(
            to_low.at[:, ys(c)], back_high.at[:, ys(c)],
            sum_send.at[1, c], sum_recv.at[1, c], {"tile": tile - 1},
        )

    def rec(k, c):
        to = peer(k)
        spot = place(c, lax.rem(to, 2)) * CHUNK
        return remote(
            recorded_hbm.at[0, :, pl.ds(pl.multiple_of(to * quarter + spot, CHUNK), CHUNK)],
            recorded.at[view, :, pl.ds(pl.multiple_of(spot, CHUNK), CHUNK)],
            rec_send.at[k - 1, c], rec_recv.at[k - 1, c], {"view": to},
        )

    def edge(ref, side, send, recv):
        up = lax.rem(odd + side, 2)
        src = pl.multiple_of(CHUNK + up * (quarter - CHUNK), CHUNK)
        dst = pl.multiple_of((1 - up) * (quarter + CHUNK), CHUNK)
        return remote(
            ref.at[:, :, pl.ds(src, CHUNK)], ref.at[:, :, pl.ds(dst, CHUNK)],
            send.at[side], recv.at[side], {"view": inner if side else outer},
        )

    def mix_edge(side):
        return edge(mixed, side, mix_send, mix_recv)

    def ratio_edge(side):
        return edge(ratios, side, ratio_send, ratio_recv)

    def start_halo(c):
        @pl.when(has_high)
        def _():
            halo_up(c).start()

        @pl.when(has_low)
        def _():
            halo_down(c).start()

    def start_rec(c):
        for k in range(1, views):
            rec(k, c).start()

    own_rows = pl.ds(pl.multiple_of(view * quarter, quarter), quarter)
    own_copy = pltpu.make_async_copy(
        recorded_hbm.at[0, :, own_rows], recorded.at[view], own_sem
    )
    own_copy.start()
    rounded[...] = estimate[...].astype(BF16)
    from_low[0:slab - HALF] = jnp.zeros_like(from_low[0:slab - HALF])
    from_high[HALF:slab] = jnp.zeros_like(from_high[HALF:slab])

    @pl.when(jnp.logical_not(has_low))
    def _():
        from_low[...] = jnp.zeros_like(from_low)
        back_low[...] = jnp.zeros_like(back_low)

    @pl.when(jnp.logical_not(has_high))
    def _():
        from_high[...] = jnp.zeros_like(from_high)
        back_high[...] = jnp.zeros_like(back_high)

    @pl.when(jnp.logical_not(has_outer))
    def _():
        rows = pl.ds(pl.multiple_of(odd * (quarter + CHUNK), CHUNK), CHUNK)
        for ref in (mixed, ratios):
            ref[:, :, rows, :] = jnp.zeros((views, slab, CHUNK, depth), BF16)

    barrier = pltpu.get_barrier_semaphore()
    for k in range(1, views):
        pl.semaphore_signal(barrier, inc=1, device_id={"view": peer(k)}, device_id_type=MESH)

    @pl.when(has_low)
    def _():
        pl.semaphore_signal(barrier, inc=1, device_id={"tile": tile - 1}, device_id_type=MESH)

    @pl.when(has_high)
    def _():
        pl.semaphore_signal(barrier, inc=1, device_id={"tile": tile + 1}, device_id_type=MESH)

    pl.semaphore_wait(
        barrier, views - 1 + has_low.astype(jnp.int32) + has_high.astype(jnp.int32)
    )
    start_halo(0)
    start_rec(0)
    start_halo(1)

    taps[...] = jnp.zeros_like(taps)
    rows, cols = slab * GROUP, 3 * slab * GROUP
    tap = lax.broadcasted_iota(jnp.int32, (taps.shape[1], cols), 0)
    spot = lax.broadcasted_iota(jnp.int32, (taps.shape[1], cols), 1)
    spread = ((spot == GROUP * (tap + slab - HALF)) & (tap < TAPS)).astype(F32).astype(BF16)
    tap = lax.broadcasted_iota(jnp.int32, (taps.shape[1], taps.shape[1]), 0)
    spot = lax.broadcasted_iota(jnp.int32, (taps.shape[1], taps.shape[1]), 1)
    mirror = ((spot == TAPS - 1 - tap) & (tap < TAPS)).astype(F32).astype(BF16)
    for s in range(views):
        lines = picked_taps(assign_ref[s], half_ref, psf_ref, taps)
        line = dot(lines.astype(BF16), spread)[0:1]
        block = pltpu.roll(jnp.broadcast_to(line, (rows, cols)), 0, 1, stride=1, stride_axis=0)
        wide_a[s * rows:(s + 1) * rows, :] = block.astype(BF16)
        wide_b[:, s * rows:(s + 1) * rows] = block.T.astype(BF16)
        cy[s] = stacked_band(lines[1:2])
        cyt[s] = stacked_band(dot(lines.astype(BF16), mirror)[1:2])
        across = band(lines[2:3], depth)
        cz[s] = across.astype(BF16)
        czt[s] = across.T.astype(BF16)
        totals = jnp.sum(lines, axis=1, keepdims=True)
        scale = 1.0 / (totals[0:1] * totals[1:2] * totals[2:3])
        scales[s:s + 1, :] = jnp.broadcast_to(scale, (1, depth))

    def blur_x(c):
        @pl.when(has_low)
        def _():
            halo_up(c).wait_recv()

        @pl.when(has_high)
        def _():
            halo_down(c).wait_recv()

        @pl.when(c + 2 < chunks)
        def _():
            start_halo(c + 2)

        cells = jnp.concatenate(
            [from_low[:, ys(c), :].astype(F32), estimate[:, ys(c), :],
             from_high[:, ys(c), :].astype(F32)], axis=0
        )
        blurs = []
        for h in range(0, CHUNK, GROUP):
            some = cells[:, h:h + GROUP, :].reshape(cols, depth).astype(BF16)
            blurs.append(dot(wide_a[...], some).reshape(views * slab, GROUP, depth))
        mixed[:, :, ys(c, CHUNK), :] = (
            jnp.concatenate(blurs, axis=1).astype(BF16).reshape(views, slab, CHUNK, depth)
        )

        @pl.when((c == 0) & has_outer)
        def _():
            mix_edge(0).start()

        @pl.when(c == chunks - 1)
        def _():
            mix_edge(1).start()

        @pl.when(c + 1 < chunks)
        def _():
            start_rec(c + 1)

    def along_y(ref, bands, s, c):
        parts = []
        for g in range(0, slab, STACK):
            data = ref[s, g:g + STACK, ys(c, 0, 3 * CHUNK), :]
            parts.append(dot(bands[s], data.reshape(3 * CHUNK * STACK, depth)).astype(BF16))
        return jnp.concatenate(parts, axis=0)

    def divide(c):
        @pl.when((c == 0) & has_outer)
        def _():
            mix_edge(0).wait_recv()

        @pl.when(c == chunks - 1)
        def _():
            mix_edge(1).wait_recv()

        @pl.when(c == 0)
        def _():
            own_copy.wait()

        for k in range(1, views):
            rec(k, c).wait_recv()
        for s in range(views):
            blurred = dot(along_y(mixed, cy, s, c), czt[s]) * scales[s:s + 1, :]
            seen = recorded[s, :, ys(c), :].astype(F32).reshape(slab * CHUNK, depth)
            ratio = (seen / blurred).astype(BF16)
            ratios[s, :, ys(c, CHUNK), :] = ratio.reshape(slab, CHUNK, depth)

        @pl.when((c == 0) & has_outer)
        def _():
            ratio_edge(0).start()

        @pl.when(c == chunks - 1)
        def _():
            ratio_edge(1).start()

    def back(c):
        @pl.when((c == 0) & has_outer)
        def _():
            ratio_edge(0).wait_recv()

        @pl.when(c == chunks - 1)
        def _():
            ratio_edge(1).wait_recv()

        halves = [[] for _ in range(0, CHUNK, GROUP)]
        for s in range(views):
            across = dot(along_y(ratios, cyt, s, c), cz[s]) * scales[s:s + 1, :]
            across = across.reshape(slab, CHUNK, depth)
            for h, half in enumerate(halves):
                some = across[:, h * GROUP:(h + 1) * GROUP, :]
                half.append(some.reshape(rows, depth).astype(BF16))
        blurs = []
        for half in halves:
            some = jnp.concatenate(half, axis=0)
            blurs.append(dot(wide_b[...], some).reshape(3 * slab, GROUP, depth))
        wide = jnp.concatenate(blurs, axis=1)
        out[:, ys(c), :] = wide[slab:2 * slab]
        for block, target, spare in (
            (wide[:slab], to_low, 0), (wide[2 * slab:], to_high, slab - 1)
        ):
            mean = (jnp.sum(block, axis=1) * (1.0 / CHUNK)).astype(BF16)
            target[:, ys(c), :] = (block - mean.astype(F32)[:, None, :]).astype(BF16)
            target[spare, ys(c), :] = mean

        @pl.when(has_high)
        def _():
            sum_up(c).start()

        @pl.when(has_low)
        def _():
            sum_down(c).start()

    def step(c, carry):
        @pl.when(c < chunks)
        def _():
            blur_x(c)

        @pl.when((c >= 1) & (c < chunks + 1))
        def _():
            divide(c - 1)

        @pl.when(c >= 2)
        def _():
            back(c - 2)

        return carry

    lax.fori_loop(0, chunks + 2, step, 0)

    def add_sums(c, carry):
        @pl.when(has_low)
        def _():
            sum_up(c).wait_recv()

        @pl.when(has_high)
        def _():
            sum_down(c).wait_recv()

        for came, spare in ((back_low, slab - 1), (back_high, 0)):
            mean = came[spare, ys(c), :].astype(F32)[:, None, :]
            added = came[:, ys(c), :].astype(F32) + mean
            for i in range(slab):
                if i != spare:
                    out[i, ys(c), :] += added[i]
        return carry

    lax.fori_loop(0, chunks, add_sums, 0)

    def wait_sends(c, carry):
        for k in range(1, views):
            rec(k, c).wait_send()

        @pl.when(has_high)
        def _():
            halo_up(c).wait_send()
            sum_up(c).wait_send()

        @pl.when(has_low)
        def _():
            halo_down(c).wait_send()
            sum_down(c).wait_send()

        return carry

    lax.fori_loop(0, chunks, wait_sends, 0)

    @pl.when(has_outer)
    def _():
        mix_edge(0).wait_send()
        ratio_edge(0).wait_send()

    mix_edge(1).wait_send()
    ratio_edge(1).wait_send()


def shards(recorded, estimate, psf_taps, half_width, assign, flags):
    views = lax.axis_size("view")
    slab, quarter, depth = estimate.shape
    chunks = quarter // CHUNK
    rows, cols = slab * GROUP, 3 * slab * GROUP
    cells = jnp.repeat(jnp.repeat(flags, 8, axis=0), 8, axis=1)[:, :, None] > 0
    vmem = pl.BlockSpec(memory_space=pltpu.VMEM)
    smem = pl.BlockSpec(memory_space=pltpu.SMEM)
    dma = pltpu.SemaphoreType.DMA
    edge = pltpu.VMEM((slab, quarter, depth), BF16)
    wide = pltpu.VMEM((views, slab, quarter + 2 * CHUNK, depth), BF16)
    total = pl.pallas_call(
        kernel,
        out_shape=jax.ShapeDtypeStruct(estimate.shape, F32),
        in_specs=[smem, smem, vmem, vmem, pl.BlockSpec(memory_space=pl.ANY)],
        out_specs=vmem,
        scratch_shapes=[
            edge,
            pltpu.VMEM((8, 256), F32),
            pltpu.VMEM((8, depth), F32),
            pltpu.VMEM((views * rows, cols), BF16),
            pltpu.VMEM((cols, views * rows), BF16),
            pltpu.VMEM((views, STACK * CHUNK, 3 * STACK * CHUNK), BF16),
            pltpu.VMEM((views, STACK * CHUNK, 3 * STACK * CHUNK), BF16),
            pltpu.VMEM((views, depth, depth), BF16),
            pltpu.VMEM((views, depth, depth), BF16),
            pltpu.VMEM((views, slab, quarter, depth), BF16),
            edge, edge,
            wide, wide,
            edge, edge, edge, edge,
            dma,
            dma((views - 1, chunks)), dma((views - 1, chunks)),
            dma((2, chunks)), dma((2, chunks)),
            dma((2,)), dma((2,)),
            dma((2,)), dma((2,)),
            dma((2, chunks)), dma((2, chunks)),
        ],
        compiler_params=pltpu.CompilerParams(collective_id=0, has_side_effects=True),
        name="deconvolve",
    )(assign, half_width.T, psf_taps.transpose(1, 0, 2), estimate, recorded)
    return jnp.where(cells, estimate * (total / views), estimate)


def solution(mesh):
    placed = (
        P("view", "tile", None, None),
        P("tile", "view", None),
        P(),
        P(),
        P(),
        P("tile", "view"),
    )
    return jax.shard_map(
        shards, mesh=mesh, in_specs=placed, out_specs=P("tile", "view", None), check_vma=False
    )
```

```python
import jax
import jax.numpy as jnp
from jax import lax
from jax.experimental import pallas as pl
from jax.experimental.pallas import tpu as pltpu
from jax.sharding import PartitionSpec as P

TAPS = 31
HALF = TAPS // 2
GROUP = 8
CHUNK = 16
STACK = 4
F32 = jnp.float32
BF16 = jnp.bfloat16
MESH = pl.DeviceIdType.MESH


def dot(a, b):
    return jnp.dot(a, b, preferred_element_type=F32)


def picked_taps(entry, half_ref, psf_ref, taps):
    for d in range(3):
        taps[d:d + 1, 0:TAPS] = psf_ref[d, pl.ds(entry, 1), :]
    row = lax.broadcasted_iota(jnp.int32, taps.shape, 0)
    col = lax.broadcasted_iota(jnp.int32, taps.shape, 1)
    width = jnp.where(
        row == 0, half_ref[0, entry], jnp.where(row == 1, half_ref[1, entry], half_ref[2, entry])
    )
    keep = (jnp.abs(col - HALF) <= width) & (col < TAPS) & (row < 3)
    return jnp.where(keep, taps[...], 0.0).astype(BF16).astype(F32)


def band(line, size):
    rolled = pltpu.roll(
        jnp.broadcast_to(line, (size, size)), size - HALF, 1, stride=1, stride_axis=0
    )
    row = lax.broadcasted_iota(jnp.int32, (size, size), 0)
    col = lax.broadcasted_iota(jnp.int32, (size, size), 1)
    return jnp.where(jnp.abs(row - col) <= HALF, rolled, 0.0)


def stacked_band(line):
    width = line.shape[1]
    blocks = [
        pltpu.roll(
            jnp.broadcast_to(line, (CHUNK, width)), 3 * CHUNK * i + CHUNK - HALF, 1,
            stride=1, stride_axis=0,
        )
        for i in range(STACK)
    ]
    return jnp.concatenate(blocks, axis=0)[:, :3 * CHUNK * STACK].astype(BF16)


def kernel(
    assign_ref, half_ref, psf_ref, estimate, recorded_hbm, out,
    rounded, taps, scales, wide_a, wide_b, cy, cyt, cz, czt, recorded,
    from_low, from_high, mixed, ratios,
    to_low, to_high, back_low, back_high,
    own_sem, rec_send, rec_recv, halo_send, halo_recv,
    mix_send, mix_recv, ratio_send, ratio_recv, sum_send, sum_recv,
):
    slab, quarter, depth = rounded.shape
    views = recorded.shape[0]
    chunks = quarter // CHUNK
    tile, view = lax.axis_index("tile"), lax.axis_index("view")
    last = lax.axis_size("tile") - 1
    has_low, has_high = tile > 0, tile < last
    odd = lax.rem(view, 2)
    inner = view + 1 - 2 * odd
    outer = view - 1 + 2 * odd
    has_outer = (outer >= 0) & (outer < views)

    def place(c, parity):
        return c + (1 - parity) * (chunks - 1 - 2 * c)

    def ys(c, base=0, size=CHUNK):
        return pl.ds(pl.multiple_of(base + place(c, odd) * CHUNK, CHUNK), size)

    def peer(k):
        return lax.rem(view + k, views)

    def remote(src, dst, send, recv, device):
        return pltpu.make_async_remote_copy(
            src_ref=src, dst_ref=dst, send_sem=send, recv_sem=recv,
            device_id=device, device_id_type=MESH,
        )

    def halo_up(c):
        return remote(
            rounded.at[slab - HALF:slab, ys(c)], from_low.at[slab - HALF:slab, ys(c)],
            halo_send.at[0, c], halo_recv.at[0, c], {"tile": tile + 1},
        )

    def halo_down(c):
        return remote(
            rounded.at[0:HALF, ys(c)], from_high.at[0:HALF, ys(c)],
            halo_send.at[1, c], halo_recv.at[1, c], {"tile": tile - 1},
        )

    def sum_up(c):
        return remote(
            to_high.at[:, ys(c)], back_low.at[:, ys(c)],
            sum_send.at[0, c], sum_recv.at[0, c], {"tile": tile + 1},
        )

    def sum_down(c):
        return remote(
            to_low.at[:, ys(c)], back_high.at[:, ys(c)],
            sum_send.at[1, c], sum_recv.at[1, c], {"tile": tile - 1},
        )

    def rec(k, c):
        to = peer(k)
        spot = place(c, lax.rem(to, 2)) * CHUNK
        return remote(
            recorded_hbm.at[0, :, pl.ds(pl.multiple_of(to * quarter + spot, CHUNK), CHUNK)],
            recorded.at[view, :, pl.ds(pl.multiple_of(spot, CHUNK), CHUNK)],
            rec_send.at[k - 1, c], rec_recv.at[k - 1, c], {"view": to},
        )

    def edge(ref, side, send, recv):
        up = lax.rem(odd + side, 2)
        src = pl.multiple_of(CHUNK + up * (quarter - CHUNK), CHUNK)
        dst = pl.multiple_of((1 - up) * (quarter + CHUNK), CHUNK)
        return remote(
            ref.at[:, :, pl.ds(src, CHUNK)], ref.at[:, :, pl.ds(dst, CHUNK)],
            send.at[side], recv.at[side], {"view": inner if side else outer},
        )

    def mix_edge(side):
        return edge(mixed, side, mix_send, mix_recv)

    def ratio_edge(side):
        return edge(ratios, side, ratio_send, ratio_recv)

    def start_halo(c):
        @pl.when(has_high)
        def _():
            halo_up(c).start()

        @pl.when(has_low)
        def _():
            halo_down(c).start()

    def start_rec(c):
        for k in range(1, views):
            rec(k, c).start()

    own_rows = pl.ds(pl.multiple_of(view * quarter, quarter), quarter)
    own_copy = pltpu.make_async_copy(
        recorded_hbm.at[0, :, own_rows], recorded.at[view], own_sem
    )
    own_copy.start()
    rounded[...] = estimate[...].astype(BF16)
    from_low[0:slab - HALF] = jnp.zeros_like(from_low[0:slab - HALF])
    from_high[HALF:slab] = jnp.zeros_like(from_high[HALF:slab])

    @pl.when(jnp.logical_not(has_low))
    def _():
        from_low[...] = jnp.zeros_like(from_low)
        back_low[...] = jnp.zeros_like(back_low)

    @pl.when(jnp.logical_not(has_high))
    def _():
        from_high[...] = jnp.zeros_like(from_high)
        back_high[...] = jnp.zeros_like(back_high)

    @pl.when(jnp.logical_not(has_outer))
    def _():
        rows = pl.ds(pl.multiple_of(odd * (quarter + CHUNK), CHUNK), CHUNK)
        for ref in (mixed, ratios):
            ref[:, :, rows, :] = jnp.zeros((views, slab, CHUNK, depth), BF16)

    barrier = pltpu.get_barrier_semaphore()
    for k in range(1, views):
        pl.semaphore_signal(barrier, inc=1, device_id={"view": peer(k)}, device_id_type=MESH)

    @pl.when(has_low)
    def _():
        pl.semaphore_signal(barrier, inc=1, device_id={"tile": tile - 1}, device_id_type=MESH)

    @pl.when(has_high)
    def _():
        pl.semaphore_signal(barrier, inc=1, device_id={"tile": tile + 1}, device_id_type=MESH)

    pl.semaphore_wait(
        barrier, views - 1 + has_low.astype(jnp.int32) + has_high.astype(jnp.int32)
    )
    start_halo(0)
    start_rec(0)
    start_halo(1)
    start_rec(1)

    taps[...] = jnp.zeros_like(taps)
    rows, cols = slab * GROUP, 3 * slab * GROUP
    tap = lax.broadcasted_iota(jnp.int32, (taps.shape[1], cols), 0)
    spot = lax.broadcasted_iota(jnp.int32, (taps.shape[1], cols), 1)
    spread = ((spot == GROUP * (tap + slab - HALF)) & (tap < TAPS)).astype(F32).astype(BF16)
    tap = lax.broadcasted_iota(jnp.int32, (taps.shape[1], taps.shape[1]), 0)
    spot = lax.broadcasted_iota(jnp.int32, (taps.shape[1], taps.shape[1]), 1)
    mirror = ((spot == TAPS - 1 - tap) & (tap < TAPS)).astype(F32).astype(BF16)
    for s in range(views):
        lines = picked_taps(assign_ref[s], half_ref, psf_ref, taps)
        line = dot(lines.astype(BF16), spread)[0:1]
        block = pltpu.roll(jnp.broadcast_to(line, (rows, cols)), 0, 1, stride=1, stride_axis=0)
        wide_a[s * rows:(s + 1) * rows, :] = block.astype(BF16)
        wide_b[:, s * rows:(s + 1) * rows] = block.T.astype(BF16)
        cy[s] = stacked_band(lines[1:2])
        cyt[s] = stacked_band(dot(lines.astype(BF16), mirror)[1:2])
        across = band(lines[2:3], depth)
        cz[s] = across.astype(BF16)
        czt[s] = across.T.astype(BF16)
        totals = jnp.sum(lines, axis=1, keepdims=True)
        scale = 1.0 / (totals[0:1] * totals[1:2] * totals[2:3])
        scales[s:s + 1, :] = jnp.broadcast_to(scale, (1, depth))

    def blur_x(c):
        @pl.when(has_low)
        def _():
            halo_up(c).wait_recv()

        @pl.when(has_high)
        def _():
            halo_down(c).wait_recv()

        @pl.when(c + 2 < chunks)
        def _():
            start_halo(c + 2)

        cells = jnp.concatenate(
            [from_low[:, ys(c), :].astype(F32), estimate[:, ys(c), :],
             from_high[:, ys(c), :].astype(F32)], axis=0
        )
        blurs = []
        for h in range(0, CHUNK, GROUP):
            some = cells[:, h:h + GROUP, :].reshape(cols, depth).astype(BF16)
            blurs.append(dot(wide_a[...], some).reshape(views * slab, GROUP, depth))
        mixed[:, :, ys(c, CHUNK), :] = (
            jnp.concatenate(blurs, axis=1).astype(BF16).reshape(views, slab, CHUNK, depth)
        )

        @pl.when(c == 0)
        def _():
            mix_edge(1).start()

        @pl.when((c == chunks - 1) & has_outer)
        def _():
            mix_edge(0).start()

        @pl.when(c + 2 < chunks)
        def _():
            start_rec(c + 2)

    def along_y(ref, bands, s, c):
        parts = []
        for g in range(0, slab, STACK):
            data = ref[s, g:g + STACK, ys(c, 0, 3 * CHUNK), :]
            parts.append(dot(bands[s], data.reshape(3 * CHUNK * STACK, depth)).astype(BF16))
        return jnp.concatenate(parts, axis=0)

    def divide(c):
        @pl.when(c == 0)
        def _():
            mix_edge(1).wait_recv()
            own_copy.wait()

        @pl.when((c == chunks - 1) & has_outer)
        def _():
            mix_edge(0).wait_recv()

        for k in range(1, views):
            rec(k, c).wait_recv()
        for s in range(views):
            blurred = dot(along_y(mixed, cy, s, c), czt[s]) * scales[s:s + 1, :]
            seen = recorded[s, :, ys(c), :].astype(F32).reshape(slab * CHUNK, depth)
            ratio = (seen / blurred).astype(BF16)
            ratios[s, :, ys(c, CHUNK), :] = ratio.reshape(slab, CHUNK, depth)

        @pl.when(c == 0)
        def _():
            ratio_edge(1).start()

        @pl.when((c == chunks - 1) & has_outer)
        def _():
            ratio_edge(0).start()

    def back(c):
        @pl.when(c == 0)
        def _():
            ratio_edge(1).wait_recv()

        @pl.when((c == chunks - 1) & has_outer)
        def _():
            ratio_edge(0).wait_recv()

        halves = [[] for _ in range(0, CHUNK, GROUP)]
        for s in range(views):
            across = dot(along_y(ratios, cyt, s, c), cz[s]) * scales[s:s + 1, :]
            across = across.reshape(slab, CHUNK, depth)
            for h, half in enumerate(halves):
                some = across[:, h * GROUP:(h + 1) * GROUP, :]
                half.append(some.reshape(rows, depth).astype(BF16))
        blurs = []
        for half in halves:
            some = jnp.concatenate(half, axis=0)
            blurs.append(dot(wide_b[...], some).reshape(3 * slab, GROUP, depth))
        wide = jnp.concatenate(blurs, axis=1)
        out[:, ys(c), :] = wide[slab:2 * slab]
        for block, target, spare in (
            (wide[:slab], to_low, 0), (wide[2 * slab:], to_high, slab - 1)
        ):
            mean = (jnp.sum(block, axis=1) * (1.0 / CHUNK)).astype(BF16)
            target[:, ys(c), :] = (block - mean.astype(F32)[:, None, :]).astype(BF16)
            target[spare, ys(c), :] = mean

        @pl.when(has_high)
        def _():
            sum_up(c).start()

        @pl.when(has_low)
        def _():
            sum_down(c).start()

    def step(c, carry):
        @pl.when(c < chunks)
        def _():
            blur_x(c)

        @pl.when((c >= 1) & (c < chunks + 1))
        def _():
            divide(c - 1)

        @pl.when(c >= 2)
        def _():
            back(c - 2)

        return carry

    lax.fori_loop(0, chunks + 2, step, 0)

    def add_sums(c, carry):
        @pl.when(has_low)
        def _():
            sum_up(c).wait_recv()

        @pl.when(has_high)
        def _():
            sum_down(c).wait_recv()

        for came, spare in ((back_low, slab - 1), (back_high, 0)):
            mean = came[spare, ys(c), :].astype(F32)[:, None, :]
            added = came[:, ys(c), :].astype(F32) + mean
            for i in range(slab):
                if i != spare:
                    out[i, ys(c), :] += added[i]
        return carry

    lax.fori_loop(0, chunks, add_sums, 0)

    def wait_sends(c, carry):
        for k in range(1, views):
            rec(k, c).wait_send()

        @pl.when(has_high)
        def _():
            halo_up(c).wait_send()
            sum_up(c).wait_send()

        @pl.when(has_low)
        def _():
            halo_down(c).wait_send()
            sum_down(c).wait_send()

        return carry

    lax.fori_loop(0, chunks, wait_sends, 0)

    @pl.when(has_outer)
    def _():
        mix_edge(0).wait_send()
        ratio_edge(0).wait_send()

    mix_edge(1).wait_send()
    ratio_edge(1).wait_send()


def shards(recorded, estimate, psf_taps, half_width, assign, flags):
    views = lax.axis_size("view")
    slab, quarter, depth = estimate.shape
    chunks = quarter // CHUNK
    rows, cols = slab * GROUP, 3 * slab * GROUP
    cells = jnp.repeat(jnp.repeat(flags, 8, axis=0), 8, axis=1)[:, :, None] > 0
    vmem = pl.BlockSpec(memory_space=pltpu.VMEM)
    smem = pl.BlockSpec(memory_space=pltpu.SMEM)
    dma = pltpu.SemaphoreType.DMA
    edge = pltpu.VMEM((slab, quarter, depth), BF16)
    wide = pltpu.VMEM((views, slab, quarter + 2 * CHUNK, depth), BF16)
    total = pl.pallas_call(
        kernel,
        out_shape=jax.ShapeDtypeStruct(estimate.shape, F32),
        in_specs=[smem, smem, vmem, vmem, pl.BlockSpec(memory_space=pl.ANY)],
        out_specs=vmem,
        scratch_shapes=[
            edge,
            pltpu.VMEM((8, 256), F32),
            pltpu.VMEM((8, depth), F32),
            pltpu.VMEM((views * rows, cols), BF16),
            pltpu.VMEM((cols, views * rows), BF16),
            pltpu.VMEM((views, STACK * CHUNK, 3 * STACK * CHUNK), BF16),
            pltpu.VMEM((views, STACK * CHUNK, 3 * STACK * CHUNK), BF16),
            pltpu.VMEM((views, depth, depth), BF16),
            pltpu.VMEM((views, depth, depth), BF16),
            pltpu.VMEM((views, slab, quarter, depth), BF16),
            edge, edge,
            wide, wide,
            edge, edge, edge, edge,
            dma,
            dma((views - 1, chunks)), dma((views - 1, chunks)),
            dma((2, chunks)), dma((2, chunks)),
            dma((2,)), dma((2,)),
            dma((2,)), dma((2,)),
            dma((2, chunks)), dma((2, chunks)),
        ],
        compiler_params=pltpu.CompilerParams(collective_id=0, has_side_effects=True),
        name="deconvolve",
    )(assign, half_width.T, psf_taps.transpose(1, 0, 2), estimate, recorded)
    return jnp.where(cells, estimate * (total / views), estimate)


def solution(mesh):
    placed = (
        P("view", "tile", None, None),
        P("tile", "view", None),
        P(),
        P(),
        P(),
        P("tile", "view"),
    )
    return jax.shard_map(
        shards, mesh=mesh, in_specs=placed, out_specs=P("tile", "view", None), check_vma=False
    )
```

```python
import jax
import jax.numpy as jnp
from jax import lax
from jax.experimental import pallas as pl
from jax.experimental.pallas import tpu as pltpu
from jax.sharding import PartitionSpec as P

TAPS = 31
HALF = TAPS // 2
GROUP = 8
CHUNK = 16
STACK = 4
F32 = jnp.float32
BF16 = jnp.bfloat16
MESH = pl.DeviceIdType.MESH


def dot(a, b):
    return jnp.dot(a, b, preferred_element_type=F32)


def picked_taps(entry, half_ref, psf_ref, taps):
    for d in range(3):
        taps[d:d + 1, 0:TAPS] = psf_ref[d, pl.ds(entry, 1), :]
    row = lax.broadcasted_iota(jnp.int32, taps.shape, 0)
    col = lax.broadcasted_iota(jnp.int32, taps.shape, 1)
    width = jnp.where(
        row == 0, half_ref[0, entry], jnp.where(row == 1, half_ref[1, entry], half_ref[2, entry])
    )
    keep = (jnp.abs(col - HALF) <= width) & (col < TAPS) & (row < 3)
    return jnp.where(keep, taps[...], 0.0).astype(BF16).astype(F32)


def band(line, size):
    rolled = pltpu.roll(
        jnp.broadcast_to(line, (size, size)), size - HALF, 1, stride=1, stride_axis=0
    )
    row = lax.broadcasted_iota(jnp.int32, (size, size), 0)
    col = lax.broadcasted_iota(jnp.int32, (size, size), 1)
    return jnp.where(jnp.abs(row - col) <= HALF, rolled, 0.0)


def stacked_band(line):
    width = line.shape[1]
    blocks = [
        pltpu.roll(
            jnp.broadcast_to(line, (CHUNK, width)), 3 * CHUNK * i + CHUNK - HALF, 1,
            stride=1, stride_axis=0,
        )
        for i in range(STACK)
    ]
    return jnp.concatenate(blocks, axis=0)[:, :3 * CHUNK * STACK].astype(BF16)


def kernel(
    assign_ref, half_ref, flags_ref, psf_ref, estimate, recorded_hbm, out,
    rounded, taps, scales, wide_a, wide_b, cy, cyt, cz, czt, recorded,
    around, mixed, ratios, center, beside,
    far_out, far_in, near_out, near_in, edge_out, edge_in,
    own_sem, rec_send, rec_recv, near_send, near_recv, pass_send, pass_recv,
    far_send, far_recv, pair_send, pair_recv, one_send, one_recv,
):
    slab, quarter, depth = estimate.shape
    views = recorded.shape[0]
    chunks = quarter // CHUNK
    tile, view = lax.axis_index("tile"), lax.axis_index("view")
    tiles = lax.axis_size("tile")
    side = lax.rem(tile, 2)
    partner = tile + 1 - 2 * side
    far_tile = tile - 2 + 4 * side
    next_tile = tile + 2 - 4 * side
    has_far = (far_tile >= 0) & (far_tile < tiles)
    has_next = (next_tile >= 0) & (next_tile < tiles)
    odd = lax.rem(view, 2)
    inner = view + 1 - 2 * odd
    outer = view - 1 + 2 * odd
    has_outer = (outer >= 0) & (outer < views)
    last = chunks + 1

    def place(c, parity):
        return c + parity * (last - 2 * c)

    def ys(c, base=0, size=CHUNK, parity=odd):
        return pl.ds(pl.multiple_of((place(c, parity) + base) * CHUNK, CHUNK), size)

    def peer(k):
        return lax.rem(view + k, views)

    def active(c):
        return (c > 0) | has_outer

    def remote(src, dst, send, recv, device):
        return pltpu.make_async_remote_copy(
            src_ref=src, dst_ref=dst, send_sem=send, recv_sem=recv,
            device_id=device, device_id_type=MESH,
        )

    def near_halo(c):
        return remote(
            rounded.at[:, ys(c)], around.at[side, :, ys(c)],
            near_send.at[c], near_recv.at[c], {"tile": partner},
        )

    def far_halo(c):
        return remote(
            around.at[1 - side, :, ys(c)], around.at[side, :, ys(c)],
            pass_send.at[c], pass_recv.at[c], {"tile": next_tile},
        )

    def far_sum(c):
        return remote(
            far_out.at[:, ys(c)], far_in.at[:, ys(c)],
            far_send.at[c], far_recv.at[c], {"tile": far_tile},
        )

    def near_sum(c):
        return remote(
            near_out.at[:, ys(c)], near_in.at[:, ys(c)],
            pair_send.at[c], pair_recv.at[c], {"tile": partner},
        )

    def rec(k, c):
        to = peer(k)
        parity = lax.rem(to, 2)
        spot = (place(c, parity) - 1) * CHUNK
        return remote(
            recorded_hbm.at[0, :, pl.ds(pl.multiple_of(to * quarter + spot, CHUNK), CHUNK)],
            recorded.at[view, :, pl.ds(pl.multiple_of(spot, CHUNK), CHUNK)],
            rec_send.at[k - 1, c - 1], rec_recv.at[k - 1, c - 1], {"view": to},
        )

    def first_edge():
        return remote(
            rounded.at[:, ys(1)], rounded.at[:, ys(0, parity=1 - odd)],
            one_send.at[0], one_recv.at[0], {"view": outer},
        )

    def last_edge():
        return remote(edge_out, edge_in, one_send.at[1], one_recv.at[1], {"view": outer})

    def mix_edge():
        return remote(
            mixed.at[:, :, ys(chunks)], mixed.at[:, :, ys(last, parity=1 - odd)],
            one_send.at[2], one_recv.at[2], {"view": inner},
        )

    def ratio_edge():
        return remote(
            ratios.at[:, :, ys(chunks, 1)], ratios.at[:, :, ys(last, 1, parity=1 - odd)],
            one_send.at[3], one_recv.at[3], {"view": inner},
        )

    def start_rec(c):
        for k in range(1, views):
            rec(k, c).start()

    own_rows = pl.ds(pl.multiple_of(view * quarter, quarter), quarter)
    own_copy = pltpu.make_async_copy(
        recorded_hbm.at[0, :, own_rows], recorded.at[view], own_sem
    )
    own_copy.start()
    rounded[:, CHUNK:CHUNK + quarter, :] = estimate[...].astype(BF16)

    @pl.when(jnp.logical_not(has_far))
    def _():
        around[side] = jnp.zeros(around.shape[1:], BF16)

    @pl.when(jnp.logical_not(has_next))
    def _():
        far_in[...] = jnp.zeros_like(far_in)

    barrier = pltpu.get_barrier_semaphore()
    for k in range(1, views):
        pl.semaphore_signal(barrier, inc=1, device_id={"view": peer(k)}, device_id_type=MESH)
    pl.semaphore_signal(barrier, inc=1, device_id={"tile": partner}, device_id_type=MESH)

    @pl.when(has_far)
    def _():
        pl.semaphore_signal(barrier, inc=1, device_id={"tile": far_tile}, device_id_type=MESH)

    @pl.when(has_next)
    def _():
        pl.semaphore_signal(barrier, inc=1, device_id={"tile": next_tile}, device_id_type=MESH)

    pl.semaphore_wait(
        barrier, views + has_far.astype(jnp.int32) + has_next.astype(jnp.int32)
    )

    @pl.when(has_outer)
    def _():
        first_edge().start()

    near_halo(1).start()
    near_halo(2).start()
    start_rec(1)
    start_rec(2)

    spare = pl.ds(pl.multiple_of(odd * (last + 1) * CHUNK, CHUNK), 2 * CHUNK)
    ratios[:, :, spare, :] = jnp.zeros((views, slab, 2 * CHUNK, depth), BF16)

    @pl.when(jnp.logical_not(has_outer))
    def _():
        mixed[:, :, ys(0), :] = jnp.zeros((views, slab, CHUNK, depth), BF16)

    taps[...] = jnp.zeros_like(taps)
    rows, cols = slab * GROUP, 3 * slab * GROUP
    tap = lax.broadcasted_iota(jnp.int32, (taps.shape[1], cols), 0)
    spot = lax.broadcasted_iota(jnp.int32, (taps.shape[1], cols), 1)
    spread = ((spot == GROUP * (tap + slab - HALF)) & (tap < TAPS)).astype(F32).astype(BF16)
    tap = lax.broadcasted_iota(jnp.int32, (taps.shape[1], taps.shape[1]), 0)
    spot = lax.broadcasted_iota(jnp.int32, (taps.shape[1], taps.shape[1]), 1)
    mirror = ((spot == TAPS - 1 - tap) & (tap < TAPS)).astype(F32).astype(BF16)
    low_rows = pl.ds(pl.multiple_of(2 * rows * side, rows), rows)
    high_rows = pl.ds(pl.multiple_of(2 * rows * (1 - side), rows), rows)
    for s in range(views):
        lines = picked_taps(assign_ref[s], half_ref, psf_ref, taps)
        line = dot(lines.astype(BF16), spread)[0:1]
        block = pltpu.roll(jnp.broadcast_to(line, (rows, cols)), 0, 1, stride=1, stride_axis=0)
        wide_a[s * rows:(s + 1) * rows, :] = block.astype(BF16)
        turned = block.T.astype(BF16)
        wide_b[low_rows, s * rows:(s + 1) * rows] = turned[:rows]
        wide_b[rows:2 * rows, s * rows:(s + 1) * rows] = turned[rows:2 * rows]
        wide_b[high_rows, s * rows:(s + 1) * rows] = turned[2 * rows:]
        cy[s] = stacked_band(lines[1:2])
        cyt[s] = stacked_band(dot(lines.astype(BF16), mirror)[1:2])
        across = band(lines[2:3], depth)
        cz[s] = across.astype(BF16)
        czt[s] = across.T.astype(BF16)
        totals = jnp.sum(lines, axis=1, keepdims=True)
        scale = 1.0 / (totals[0:1] * totals[1:2] * totals[2:3])
        scales[s:s + 1, :] = jnp.broadcast_to(scale, (1, depth))

    @pl.when(has_outer)
    def _():
        first_edge().wait_recv()
        near_halo(0).start()

    def pass_on(c):
        near_halo(c).wait_recv()

        @pl.when(has_next)
        def _():
            far_halo(c).start()

    def blur_x(c):
        @pl.when(has_far)
        def _():
            far_halo(c).wait_recv()

        cells = jnp.concatenate(
            [around[0, :, ys(c), :], rounded[:, ys(c), :], around[1, :, ys(c), :]], axis=0
        ).astype(F32)
        blurs = []
        for h in range(0, CHUNK, GROUP):
            some = cells[:, h:h + GROUP, :].reshape(cols, depth).astype(BF16)
            blurs.append(dot(wide_a[...], some).reshape(views * slab, GROUP, depth))
        mixed[:, :, ys(c), :] = (
            jnp.concatenate(blurs, axis=1).astype(BF16).reshape(views, slab, CHUNK, depth)
        )

        @pl.when(c == chunks)
        def _():
            mix_edge().start()

    def along_y(ref, bands, s, c, base):
        parts = []
        for g in range(0, slab, STACK):
            data = ref[s, g:g + STACK, ys(c, base, 3 * CHUNK), :]
            parts.append(dot(bands[s], data.reshape(3 * CHUNK * STACK, depth)).astype(BF16))
        return jnp.concatenate(parts, axis=0)

    def divide(c):
        @pl.when(c == 1)
        def _():
            own_copy.wait()

        @pl.when(c == chunks)
        def _():
            mix_edge().wait_recv()

        for k in range(1, views):
            rec(k, c).wait_recv()

        @pl.when(c + 2 <= chunks)
        def _():
            start_rec(c + 2)

        for s in range(views):
            blurred = dot(along_y(mixed, cy, s, c, -1), czt[s]) * scales[s:s + 1, :]
            seen = recorded[s, :, ys(c, -1), :].astype(F32).reshape(slab * CHUNK, depth)
            ratio = (seen / blurred).astype(BF16)
            ratios[s, :, ys(c, 1), :] = ratio.reshape(slab, CHUNK, depth)

        @pl.when(c == chunks)
        def _():
            ratio_edge().start()

    def packed(block, target, rows):
        mean = (jnp.sum(block, axis=1) * (1.0 / CHUNK)).astype(BF16)
        target[0:slab, rows, :] = (block - mean.astype(F32)[:, None, :]).astype(BF16)
        target[slab, rows, :] = mean

    def unpacked(source, rows):
        mean = source[slab, rows, :].astype(F32)[:, None, :]
        return source[0:slab, rows, :].astype(F32) + mean

    def back(c):
        @pl.when(c == chunks)
        def _():
            ratio_edge().wait_recv()

        halves = [[] for _ in range(0, CHUNK, GROUP)]
        for s in range(views):
            across = dot(along_y(ratios, cyt, s, c, 0), cz[s]) * scales[s:s + 1, :]
            across = across.reshape(slab, CHUNK, depth)
            for h, half in enumerate(halves):
                some = across[:, h * GROUP:(h + 1) * GROUP, :]
                half.append(some.reshape(rows, depth).astype(BF16))
        blurs = []
        for half in halves:
            some = jnp.concatenate(half, axis=0)
            blurs.append(dot(wide_b[...], some).reshape(3 * slab, GROUP, depth))
        wide = jnp.concatenate(blurs, axis=1)
        packed(wide[:slab], far_out, ys(c))

        @pl.when(has_far)
        def _():
            far_sum(c).start()

        center[:, ys(c), :] = wide[slab:2 * slab]
        beside[:, ys(c), :] = wide[2 * slab:]

    def combine(c):
        @pl.when(has_next)
        def _():
            far_sum(c).wait_recv()

        packed(beside[:, ys(c), :] + unpacked(far_in, ys(c)), near_out, ys(c))
        near_sum(c).start()

    def finish(c):
        near_sum(c).wait_recv()
        center[:, ys(c), :] += unpacked(near_in, ys(c))

        @pl.when(c == 0)
        def _():
            packed(center[:, ys(0), :], edge_out, slice(0, CHUNK))
            last_edge().start()

        @pl.when((c == 1) & has_outer)
        def _():
            last_edge().wait_recv()
            center[:, ys(1), :] += unpacked(edge_in, slice(0, CHUNK))

        @pl.when(c > 0)
        def _():
            spot = place(c, odd)
            for i in range(0, slab, GROUP):
                for h in range(CHUNK // GROUP):
                    near = pl.ds(pl.multiple_of(spot * CHUNK + h * GROUP, GROUP), GROUP)
                    here = pl.ds(pl.multiple_of((spot - 1) * CHUNK + h * GROUP, GROUP), GROUP)
                    flag = flags_ref[i // GROUP, (spot - 1) * (CHUNK // GROUP) + h]
                    was = estimate[i:i + GROUP, here, :]
                    now = was * (center[i:i + GROUP, near, :] * (1.0 / views))
                    out[i:i + GROUP, here, :] = jnp.where(flag > 0, now, was)

    def step(j, carry):
        def at(first, count, body, order=lambda c: c):
            c = order(j - first)

            @pl.when((j >= first) & (j < first + count) & active(c))
            def _():
                body(c)

        def early(c):
            return c + (c < 2).astype(jnp.int32) * (1 - 2 * c)

        @pl.when(j + 3 <= chunks)
        def _():
            near_halo(j + 3).start()

        at(0, chunks + 1, pass_on, early)
        at(1, chunks + 1, blur_x, early)
        at(3, chunks, divide, lambda c: c + 1)
        at(3, chunks + 1, back)
        at(4, chunks + 1, combine)
        at(5, chunks + 1, finish)
        return carry

    lax.fori_loop(0, chunks + 6, step, 0)

    def wait_sends(c, carry):
        @pl.when(active(c))
        def _():
            near_halo(c).wait_send()
            near_sum(c).wait_send()

            @pl.when(has_next)
            def _():
                far_halo(c).wait_send()

            @pl.when(has_far)
            def _():
                far_sum(c).wait_send()

        @pl.when(c > 0)
        def _():
            for k in range(1, views):
                rec(k, c).wait_send()

        return carry

    lax.fori_loop(0, chunks + 1, wait_sends, 0)

    @pl.when(has_outer)
    def _():
        first_edge().wait_send()
        last_edge().wait_send()

    mix_edge().wait_send()
    ratio_edge().wait_send()


def shards(recorded, estimate, psf_taps, half_width, assign, flags):
    views = lax.axis_size("view")
    slab, quarter, depth = estimate.shape
    chunks = quarter // CHUNK
    rows, cols = slab * GROUP, 3 * slab * GROUP
    vmem = pl.BlockSpec(memory_space=pltpu.VMEM)
    smem = pl.BlockSpec(memory_space=pltpu.SMEM)
    dma = pltpu.SemaphoreType.DMA
    reach = quarter + 2 * CHUNK
    sums = pltpu.VMEM((slab + 1, reach, depth), BF16)
    edge = pltpu.VMEM((slab + 1, CHUNK, depth), BF16)
    total = pltpu.VMEM((slab, reach, depth), F32)
    each = dma((chunks + 1,))
    return pl.pallas_call(
        kernel,
        out_shape=jax.ShapeDtypeStruct(estimate.shape, F32),
        in_specs=[smem, smem, smem, vmem, vmem, pl.BlockSpec(memory_space=pl.ANY)],
        out_specs=vmem,
        scratch_shapes=[
            pltpu.VMEM((slab, reach, depth), BF16),
            pltpu.VMEM((8, 256), F32),
            pltpu.VMEM((8, depth), F32),
            pltpu.VMEM((views * rows, cols), BF16),
            pltpu.VMEM((cols, views * rows), BF16),
            pltpu.VMEM((views, STACK * CHUNK, 3 * STACK * CHUNK), BF16),
            pltpu.VMEM((views, STACK * CHUNK, 3 * STACK * CHUNK), BF16),
            pltpu.VMEM((views, depth, depth), BF16),
            pltpu.VMEM((views, depth, depth), BF16),
            pltpu.VMEM((views, slab, quarter, depth), BF16),
            pltpu.VMEM((2, slab, reach, depth), BF16),
            pltpu.VMEM((views, slab, reach, depth), BF16),
            pltpu.VMEM((views, slab, reach + 2 * CHUNK, depth), BF16),
            total, total,
            sums, sums, sums, sums, edge, edge,
            dma,
            dma((views - 1, chunks)), dma((views - 1, chunks)),
            each, each, each, each, each, each, each, each,
            dma((4,)), dma((4,)),
        ],
        compiler_params=pltpu.CompilerParams(collective_id=0, has_side_effects=True),
        name="deconvolve",
    )(assign, half_width.T, flags, psf_taps.transpose(1, 0, 2), estimate, recorded)


def solution(mesh):
    placed = (
        P("view", "tile", None, None),
        P("tile", "view", None),
        P(),
        P(),
        P(),
        P("tile", "view"),
    )
    return jax.shard_map(
        shards, mesh=mesh, in_specs=placed, out_specs=P("tile", "view", None), check_vma=False
    )
```

```python
import jax
import jax.numpy as jnp
from jax import lax
from jax.experimental import pallas as pl
from jax.experimental.pallas import tpu as pltpu
from jax.sharding import PartitionSpec as P

TAPS = 31
HALF = TAPS // 2
GROUP = 8
CHUNK = 16
STACK = 4
VMEM_LIMIT = 40 << 20
F32 = jnp.float32
BF16 = jnp.bfloat16
MESH = pl.DeviceIdType.MESH


def dot(a, b):
    return jnp.dot(a, b, preferred_element_type=F32)


def picked_taps(entry, half_ref, psf_ref, taps):
    for d in range(3):
        taps[d:d + 1, 0:TAPS] = psf_ref[d, pl.ds(entry, 1), :]
    row = lax.broadcasted_iota(jnp.int32, taps.shape, 0)
    col = lax.broadcasted_iota(jnp.int32, taps.shape, 1)
    width = jnp.where(
        row == 0, half_ref[0, entry], jnp.where(row == 1, half_ref[1, entry], half_ref[2, entry])
    )
    keep = (jnp.abs(col - HALF) <= width) & (col < TAPS) & (row < 3)
    return jnp.where(keep, taps[...], 0.0).astype(BF16).astype(F32)


def band(line, size):
    rolled = pltpu.roll(
        jnp.broadcast_to(line, (size, size)), size - HALF, 1, stride=1, stride_axis=0
    )
    row = lax.broadcasted_iota(jnp.int32, (size, size), 0)
    col = lax.broadcasted_iota(jnp.int32, (size, size), 1)
    return jnp.where(jnp.abs(row - col) <= HALF, rolled, 0.0)


def stacked_band(line):
    width = line.shape[1]
    blocks = [
        pltpu.roll(
            jnp.broadcast_to(line, (CHUNK, width)), 3 * CHUNK * i + CHUNK - HALF, 1,
            stride=1, stride_axis=0,
        )
        for i in range(STACK)
    ]
    return jnp.concatenate(blocks, axis=0)[:, :3 * CHUNK * STACK].astype(BF16)


def kernel(
    assign_hbm, half_hbm, flags_hbm, psf_hbm, estimate_hbm, recorded_hbm, out,
    assign_ref, half_ref, flags_ref, psf_ref, estimate,
    rounded, taps, scales, wide_a, wide_b, cy, cyt, cz, czt, recorded,
    around, mixed, ratios, center, beside,
    far_out, far_in, near_out, near_in, edge_out, edge_in,
    in_sem, own_sem, rec_send, rec_recv, near_send, near_recv, pass_send, pass_recv,
    far_send, far_recv, pair_send, pair_recv, one_send, one_recv,
):
    slab, quarter, depth = estimate.shape
    views = recorded.shape[0]
    chunks = quarter // CHUNK
    tile, view = lax.axis_index("tile"), lax.axis_index("view")
    tiles = lax.axis_size("tile")
    side = lax.rem(tile, 2)
    partner = tile + 1 - 2 * side
    far_tile = tile - 2 + 4 * side
    next_tile = tile + 2 - 4 * side
    has_far = (far_tile >= 0) & (far_tile < tiles)
    has_next = (next_tile >= 0) & (next_tile < tiles)
    odd = lax.rem(view, 2)
    inner = view + 1 - 2 * odd
    outer = view - 1 + 2 * odd
    has_outer = (outer >= 0) & (outer < views)
    last = chunks + 1

    def place(c, parity):
        return c + parity * (last - 2 * c)

    def ys(c, base=0, size=CHUNK, parity=odd):
        return pl.ds(pl.multiple_of((place(c, parity) + base) * CHUNK, CHUNK), size)

    def peer(k):
        return lax.rem(view + k, views)

    def active(c):
        return (c > 0) | has_outer

    def remote(src, dst, send, recv, device):
        return pltpu.make_async_remote_copy(
            src_ref=src, dst_ref=dst, send_sem=send, recv_sem=recv,
            device_id=device, device_id_type=MESH,
        )

    def near_halo(c):
        return remote(
            rounded.at[:, ys(c)], around.at[side, :, ys(c)],
            near_send.at[c], near_recv.at[c], {"tile": partner},
        )

    def far_halo(c):
        return remote(
            around.at[1 - side, :, ys(c)], around.at[side, :, ys(c)],
            pass_send.at[c], pass_recv.at[c], {"tile": next_tile},
        )

    def far_sum(c):
        return remote(
            far_out.at[:, ys(c)], far_in.at[:, ys(c)],
            far_send.at[c], far_recv.at[c], {"tile": far_tile},
        )

    def near_sum(c):
        return remote(
            near_out.at[:, ys(c)], near_in.at[:, ys(c)],
            pair_send.at[c], pair_recv.at[c], {"tile": partner},
        )

    def rec(k, c):
        to = peer(k)
        parity = lax.rem(to, 2)
        spot = (place(c, parity) - 1) * CHUNK
        return remote(
            recorded_hbm.at[0, :, pl.ds(pl.multiple_of(to * quarter + spot, CHUNK), CHUNK)],
            recorded.at[view, :, pl.ds(pl.multiple_of(spot, CHUNK), CHUNK)],
            rec_send.at[k - 1, c - 1], rec_recv.at[k - 1, c - 1], {"view": to},
        )

    def first_edge():
        return remote(
            rounded.at[:, ys(1)], rounded.at[:, ys(0, parity=1 - odd)],
            one_send.at[0], one_recv.at[0], {"view": outer},
        )

    def last_edge():
        return remote(edge_out, edge_in, one_send.at[1], one_recv.at[1], {"view": outer})

    def mix_edge():
        return remote(
            mixed.at[:, :, ys(chunks)], mixed.at[:, :, ys(last, parity=1 - odd)],
            one_send.at[2], one_recv.at[2], {"view": inner},
        )

    def ratio_edge():
        return remote(
            ratios.at[:, :, ys(chunks, 1)], ratios.at[:, :, ys(last, 1, parity=1 - odd)],
            one_send.at[3], one_recv.at[3], {"view": inner},
        )

    def start_rec(c):
        for k in range(1, views):
            rec(k, c).start()

    own_rows = pl.ds(pl.multiple_of(view * quarter, quarter), quarter)
    own_copy = pltpu.make_async_copy(
        recorded_hbm.at[0, :, own_rows], recorded.at[view], own_sem
    )
    ins = [
        pltpu.make_async_copy(src, dst, in_sem.at[i])
        for i, (src, dst) in enumerate((
            (estimate_hbm, estimate), (psf_hbm, psf_ref), (assign_hbm, assign_ref),
            (half_hbm, half_ref), (flags_hbm, flags_ref),
        ))
    ]
    for copy in ins:
        copy.start()
    barrier = pltpu.get_barrier_semaphore()
    for k in range(1, views):
        pl.semaphore_signal(barrier, inc=1, device_id={"view": peer(k)}, device_id_type=MESH)
    pl.semaphore_signal(barrier, inc=1, device_id={"tile": partner}, device_id_type=MESH)

    @pl.when(has_far)
    def _():
        pl.semaphore_signal(barrier, inc=1, device_id={"tile": far_tile}, device_id_type=MESH)

    @pl.when(has_next)
    def _():
        pl.semaphore_signal(barrier, inc=1, device_id={"tile": next_tile}, device_id_type=MESH)

    own_copy.start()
    ins[0].wait()
    rounded[:, CHUNK:CHUNK + quarter, :] = estimate[...].astype(BF16)
    pl.semaphore_wait(
        barrier, views + has_far.astype(jnp.int32) + has_next.astype(jnp.int32)
    )

    @pl.when(has_outer)
    def _():
        first_edge().start()

    near_halo(1).start()
    start_rec(1)
    start_rec(2)

    @pl.when(jnp.logical_not(has_far))
    def _():
        around[side] = jnp.zeros(around.shape[1:], BF16)

    @pl.when(jnp.logical_not(has_next))
    def _():
        far_in[...] = jnp.zeros_like(far_in)

    spare = pl.ds(pl.multiple_of(odd * (last + 1) * CHUNK, CHUNK), 2 * CHUNK)
    ratios[:, :, spare, :] = jnp.zeros((views, slab, 2 * CHUNK, depth), BF16)

    @pl.when(jnp.logical_not(has_outer))
    def _():
        mixed[:, :, ys(0), :] = jnp.zeros((views, slab, CHUNK, depth), BF16)

    taps[...] = jnp.zeros_like(taps)
    for copy in ins[1:]:
        copy.wait()
    rows, cols = slab * GROUP, 3 * slab * GROUP
    tap = lax.broadcasted_iota(jnp.int32, (taps.shape[1], cols), 0)
    spot = lax.broadcasted_iota(jnp.int32, (taps.shape[1], cols), 1)
    spread = ((spot == GROUP * (tap + slab - HALF)) & (tap < TAPS)).astype(F32).astype(BF16)
    tap = lax.broadcasted_iota(jnp.int32, (taps.shape[1], taps.shape[1]), 0)
    spot = lax.broadcasted_iota(jnp.int32, (taps.shape[1], taps.shape[1]), 1)
    mirror = ((spot == TAPS - 1 - tap) & (tap < TAPS)).astype(F32).astype(BF16)
    low_rows = pl.ds(pl.multiple_of(2 * rows * side, rows), rows)
    high_rows = pl.ds(pl.multiple_of(2 * rows * (1 - side), rows), rows)
    for s in range(views):
        lines = picked_taps(assign_ref[s], half_ref, psf_ref, taps)
        line = dot(lines.astype(BF16), spread)[0:1]
        block = pltpu.roll(jnp.broadcast_to(line, (rows, cols)), 0, 1, stride=1, stride_axis=0)
        wide_a[s * rows:(s + 1) * rows, :] = block.astype(BF16)
        turned = block.T.astype(BF16)
        wide_b[low_rows, s * rows:(s + 1) * rows] = turned[:rows]
        wide_b[rows:2 * rows, s * rows:(s + 1) * rows] = turned[rows:2 * rows]
        wide_b[high_rows, s * rows:(s + 1) * rows] = turned[2 * rows:]
        cy[s] = stacked_band(lines[1:2])
        cyt[s] = stacked_band(dot(lines.astype(BF16), mirror)[1:2])
        across = band(lines[2:3], depth)
        cz[s] = across.astype(BF16)
        czt[s] = across.T.astype(BF16)
        totals = jnp.sum(lines, axis=1, keepdims=True)
        scale = 1.0 / (totals[0:1] * totals[1:2] * totals[2:3])
        scales[s:s + 1, :] = jnp.broadcast_to(scale, (1, depth))

    @pl.when(has_outer)
    def _():
        first_edge().wait_recv()
        near_halo(0).start()

    def pass_on(c):
        near_halo(c).wait_recv()

        @pl.when(has_next)
        def _():
            far_halo(c).start()

    def blur_x(c):
        @pl.when(has_far)
        def _():
            far_halo(c).wait_recv()

        cells = jnp.concatenate(
            [around[0, :, ys(c), :], rounded[:, ys(c), :], around[1, :, ys(c), :]], axis=0
        ).astype(F32)
        blurs = []
        for h in range(0, CHUNK, GROUP):
            some = cells[:, h:h + GROUP, :].reshape(cols, depth).astype(BF16)
            blurs.append(dot(wide_a[...], some).reshape(views * slab, GROUP, depth))
        mixed[:, :, ys(c), :] = (
            jnp.concatenate(blurs, axis=1).astype(BF16).reshape(views, slab, CHUNK, depth)
        )

        @pl.when(c == chunks)
        def _():
            mix_edge().start()

    def along_y(ref, bands, s, c, base):
        parts = []
        for g in range(0, slab, STACK):
            data = ref[s, g:g + STACK, ys(c, base, 3 * CHUNK), :]
            parts.append(dot(bands[s], data.reshape(3 * CHUNK * STACK, depth)).astype(BF16))
        return jnp.concatenate(parts, axis=0)

    def divide(c):
        @pl.when(c == 1)
        def _():
            own_copy.wait()

        @pl.when(c == chunks)
        def _():
            mix_edge().wait_recv()

        for k in range(1, views):
            rec(k, c).wait_recv()

        @pl.when(c + 2 <= chunks)
        def _():
            start_rec(c + 2)

        for s in range(views):
            blurred = dot(along_y(mixed, cy, s, c, -1), czt[s]) * scales[s:s + 1, :]
            seen = recorded[s, :, ys(c, -1), :].astype(F32).reshape(slab * CHUNK, depth)
            ratio = (seen / blurred).astype(BF16)
            ratios[s, :, ys(c, 1), :] = ratio.reshape(slab, CHUNK, depth)

        @pl.when(c == chunks)
        def _():
            ratio_edge().start()

    def packed(block, target, rows):
        mean = (jnp.sum(block, axis=1) * (1.0 / CHUNK)).astype(BF16)
        target[0:slab, rows, :] = (block - mean.astype(F32)[:, None, :]).astype(BF16)
        target[slab, rows, :] = mean

    def unpacked(source, rows):
        mean = source[slab, rows, :].astype(F32)[:, None, :]
        return source[0:slab, rows, :].astype(F32) + mean

    def back(c):
        @pl.when(c == chunks)
        def _():
            ratio_edge().wait_recv()

        halves = [[] for _ in range(0, CHUNK, GROUP)]
        for s in range(views):
            across = dot(along_y(ratios, cyt, s, c, 0), cz[s]) * scales[s:s + 1, :]
            across = across.reshape(slab, CHUNK, depth)
            for h, half in enumerate(halves):
                some = across[:, h * GROUP:(h + 1) * GROUP, :]
                half.append(some.reshape(rows, depth).astype(BF16))
        blurs = []
        for half in halves:
            some = jnp.concatenate(half, axis=0)
            blurs.append(dot(wide_b[...], some).reshape(3 * slab, GROUP, depth))
        wide = jnp.concatenate(blurs, axis=1)
        packed(wide[:slab], far_out, ys(c))

        @pl.when(has_far)
        def _():
            far_sum(c).start()

        center[:, ys(c), :] = wide[slab:2 * slab]
        beside[:, ys(c), :] = wide[2 * slab:]

    def combine(c):
        @pl.when(has_next)
        def _():
            far_sum(c).wait_recv()

        packed(beside[:, ys(c), :] + unpacked(far_in, ys(c)), near_out, ys(c))
        near_sum(c).start()

    def finish(c):
        near_sum(c).wait_recv()
        center[:, ys(c), :] += unpacked(near_in, ys(c))

        @pl.when(c == 0)
        def _():
            packed(center[:, ys(0), :], edge_out, slice(0, CHUNK))
            last_edge().start()

        @pl.when((c == 1) & has_outer)
        def _():
            last_edge().wait_recv()
            center[:, ys(1), :] += unpacked(edge_in, slice(0, CHUNK))

        @pl.when(c > 0)
        def _():
            spot = place(c, odd)
            for i in range(0, slab, GROUP):
                for h in range(CHUNK // GROUP):
                    near = pl.ds(pl.multiple_of(spot * CHUNK + h * GROUP, GROUP), GROUP)
                    here = pl.ds(pl.multiple_of((spot - 1) * CHUNK + h * GROUP, GROUP), GROUP)
                    flag = flags_ref[i // GROUP, (spot - 1) * (CHUNK // GROUP) + h]
                    was = estimate[i:i + GROUP, here, :]
                    now = was * (center[i:i + GROUP, near, :] * (1.0 / views))
                    out[i:i + GROUP, here, :] = jnp.where(flag > 0, now, was)

    def step(j, carry):
        def at(first, count, body, order=lambda c: c):
            c = order(j - first)

            @pl.when((j >= first) & (j < first + count) & active(c))
            def _():
                body(c)

        def early(c):
            return c + (c < 2).astype(jnp.int32) * (1 - 2 * c)

        @pl.when((j >= 1) & (j + 1 <= chunks))
        def _():
            near_halo(j + 1).start()

        at(0, chunks + 1, pass_on, early)
        at(1, chunks + 1, blur_x, early)
        at(3, chunks, divide, lambda c: c + 1)
        at(3, chunks + 1, back)
        at(4, chunks + 1, combine)
        at(5, chunks + 1, finish)
        return carry

    lax.fori_loop(0, chunks + 6, step, 0)

    def wait_sends(c, carry):
        @pl.when(active(c))
        def _():
            near_halo(c).wait_send()
            near_sum(c).wait_send()

            @pl.when(has_next)
            def _():
                far_halo(c).wait_send()

            @pl.when(has_far)
            def _():
                far_sum(c).wait_send()

        @pl.when(c > 0)
        def _():
            for k in range(1, views):
                rec(k, c).wait_send()

        return carry

    lax.fori_loop(0, chunks + 1, wait_sends, 0)

    @pl.when(has_outer)
    def _():
        first_edge().wait_send()
        last_edge().wait_send()

    mix_edge().wait_send()
    ratio_edge().wait_send()


def shards(recorded, estimate, psf_taps, half_width, assign, flags):
    views = lax.axis_size("view")
    slab, quarter, depth = estimate.shape
    chunks = quarter // CHUNK
    rows, cols = slab * GROUP, 3 * slab * GROUP
    hbm = pl.BlockSpec(memory_space=pltpu.HBM)
    half_width, psf_taps = half_width.T, psf_taps.transpose(1, 0, 2)
    dma = pltpu.SemaphoreType.DMA
    reach = quarter + 2 * CHUNK
    sums = pltpu.VMEM((slab + 1, reach, depth), BF16)
    edge = pltpu.VMEM((slab + 1, CHUNK, depth), BF16)
    total = pltpu.VMEM((slab, reach, depth), F32)
    each = dma((chunks + 1,))
    return pl.pallas_call(
        kernel,
        out_shape=jax.ShapeDtypeStruct(estimate.shape, F32),
        in_specs=[hbm] * 6,
        out_specs=pl.BlockSpec(memory_space=pltpu.VMEM),
        scratch_shapes=[
            pltpu.SMEM(assign.shape, assign.dtype),
            pltpu.SMEM(half_width.shape, half_width.dtype),
            pltpu.SMEM(flags.shape, flags.dtype),
            pltpu.VMEM(psf_taps.shape, F32),
            pltpu.VMEM(estimate.shape, F32),
            pltpu.VMEM((slab, reach, depth), BF16),
            pltpu.VMEM((8, 256), F32),
            pltpu.VMEM((8, depth), F32),
            pltpu.VMEM((views * rows, cols), BF16),
            pltpu.VMEM((cols, views * rows), BF16),
            pltpu.VMEM((views, STACK * CHUNK, 3 * STACK * CHUNK), BF16),
            pltpu.VMEM((views, STACK * CHUNK, 3 * STACK * CHUNK), BF16),
            pltpu.VMEM((views, depth, depth), BF16),
            pltpu.VMEM((views, depth, depth), BF16),
            pltpu.VMEM((views, slab, quarter, depth), BF16),
            pltpu.VMEM((2, slab, reach, depth), BF16),
            pltpu.VMEM((views, slab, reach, depth), BF16),
            pltpu.VMEM((views, slab, reach + 2 * CHUNK, depth), BF16),
            total, total,
            sums, sums, sums, sums, edge, edge,
            dma((5,)), dma,
            dma((views - 1, chunks)), dma((views - 1, chunks)),
            each, each, each, each, each, each, each, each,
            dma((4,)), dma((4,)),
        ],
        compiler_params=pltpu.CompilerParams(
            collective_id=0, has_side_effects=True, vmem_limit_bytes=VMEM_LIMIT
        ),
        name="deconvolve",
    )(*(
        pltpu.with_memory_space_constraint(a, pltpu.HBM)
        for a in (assign, half_width, flags, psf_taps, estimate, recorded)
    ))


def solution(mesh):
    placed = (
        P("view", "tile", None, None),
        P("tile", "view", None),
        P(),
        P(),
        P(),
        P("tile", "view"),
    )
    return jax.shard_map(
        shards, mesh=mesh, in_specs=placed, out_specs=P("tile", "view", None), check_vma=False
    )
```

```python
import jax
import jax.numpy as jnp
from jax import lax
from jax.experimental import pallas as pl
from jax.experimental.pallas import tpu as pltpu
from jax.sharding import PartitionSpec as P

TAPS = 31
HALF = TAPS // 2
GROUP = 8
CHUNK = 16
STACK = 4
LANES = 128
VMEM_LIMIT = 40 << 20
F32 = jnp.float32
BF16 = jnp.bfloat16
MESH = pl.DeviceIdType.MESH


def dot(a, b):
    return jnp.dot(a, b, preferred_element_type=F32)


def picked_taps(entry, half_ref, psf_ref, taps):
    for d in range(3):
        taps[d:d + 1, 0:TAPS] = psf_ref[d, pl.ds(entry, 1), :]
    row = lax.broadcasted_iota(jnp.int32, taps.shape, 0)
    col = lax.broadcasted_iota(jnp.int32, taps.shape, 1)
    width = jnp.where(
        row == 0, half_ref[0, entry], jnp.where(row == 1, half_ref[1, entry], half_ref[2, entry])
    )
    keep = (jnp.abs(col - HALF) <= width) & (col < TAPS) & (row < 3)
    return jnp.where(keep, taps[...], 0.0).astype(BF16).astype(F32)


def band(line, size):
    rolled = pltpu.roll(
        jnp.broadcast_to(line, (size, size)), size - HALF, 1, stride=1, stride_axis=0
    )
    row = lax.broadcasted_iota(jnp.int32, (size, size), 0)
    col = lax.broadcasted_iota(jnp.int32, (size, size), 1)
    return jnp.where(jnp.abs(row - col) <= HALF, rolled, 0.0)


def stacked_band(line):
    width = line.shape[1]
    blocks = [
        pltpu.roll(
            jnp.broadcast_to(line, (CHUNK, width)), 3 * CHUNK * i + CHUNK - HALF, 1,
            stride=1, stride_axis=0,
        )
        for i in range(STACK)
    ]
    return jnp.concatenate(blocks, axis=0)[:, :3 * CHUNK * STACK].astype(BF16)


def kernel(
    assign_hbm, half_hbm, flags_hbm, psf_hbm, estimate_hbm, recorded_hbm, out,
    assign_ref, half_ref, flags_ref, psf_ref, estimate,
    rounded, taps, scales, wide_a, wide_b, cy, cyt, cz, czt, recorded,
    around, mixed, ratios, center, beside,
    far_out, far_in, near_out, near_in, edge_out, edge_in,
    in_sem, own_sem, rec_send, rec_recv, near_send, near_recv, pass_send, pass_recv,
    far_send, far_recv, pair_send, pair_recv, one_send, one_recv,
):
    slab, quarter, depth = estimate.shape
    views = recorded.shape[0]
    chunks = quarter // CHUNK
    pieces = depth // LANES
    tile, view = lax.axis_index("tile"), lax.axis_index("view")
    tiles = lax.axis_size("tile")
    side = lax.rem(tile, 2)
    partner = tile + 1 - 2 * side
    far_tile = tile - 2 + 4 * side
    next_tile = tile + 2 - 4 * side
    has_far = (far_tile >= 0) & (far_tile < tiles)
    has_next = (next_tile >= 0) & (next_tile < tiles)
    odd = lax.rem(view, 2)
    inner = view + 1 - 2 * odd
    outer = view - 1 + 2 * odd
    has_outer = (outer >= 0) & (outer < views)
    last = chunks + 1

    def place(c, parity):
        return c + parity * (last - 2 * c)

    def ys(c, base=0, size=CHUNK, parity=odd):
        return pl.ds(pl.multiple_of((place(c, parity) + base) * CHUNK, CHUNK), size)

    def peer(k):
        return lax.rem(view + k, views)

    def active(c):
        return (c > 0) | has_outer

    def remote(src, dst, send, recv, device):
        return pltpu.make_async_remote_copy(
            src_ref=src, dst_ref=dst, send_sem=send, recv_sem=recv,
            device_id=device, device_id_type=MESH,
        )

    def zs(p):
        return slice(p * LANES, (p + 1) * LANES)

    def near_halo(c, p):
        return remote(
            rounded.at[:, ys(c), zs(p)], around.at[side, :, ys(c), zs(p)],
            near_send.at[p, c], near_recv.at[p, c], {"tile": partner},
        )

    def far_halo(c, p):
        return remote(
            around.at[1 - side, :, ys(c), zs(p)], around.at[side, :, ys(c), zs(p)],
            pass_send.at[p, c], pass_recv.at[p, c], {"tile": next_tile},
        )

    def far_sum(c, p):
        return remote(
            far_out.at[:, ys(c), zs(p)], far_in.at[:, ys(c), zs(p)],
            far_send.at[p, c], far_recv.at[p, c], {"tile": far_tile},
        )

    def near_sum(c, p):
        return remote(
            near_out.at[:, ys(c), zs(p)], near_in.at[:, ys(c), zs(p)],
            pair_send.at[p, c], pair_recv.at[p, c], {"tile": partner},
        )

    def rec(k, c):
        to = peer(k)
        parity = lax.rem(to, 2)
        spot = (place(c, parity) - 1) * CHUNK
        return remote(
            recorded_hbm.at[0, :, pl.ds(pl.multiple_of(to * quarter + spot, CHUNK), CHUNK)],
            recorded.at[view, :, pl.ds(pl.multiple_of(spot, CHUNK), CHUNK)],
            rec_send.at[k - 1, c - 1], rec_recv.at[k - 1, c - 1], {"view": to},
        )

    def first_edge():
        return remote(
            rounded.at[:, ys(1)], rounded.at[:, ys(0, parity=1 - odd)],
            one_send.at[0], one_recv.at[0], {"view": outer},
        )

    def last_edge():
        return remote(edge_out, edge_in, one_send.at[1], one_recv.at[1], {"view": outer})

    def mix_edge():
        return remote(
            mixed.at[:, :, ys(chunks)], mixed.at[:, :, ys(last, parity=1 - odd)],
            one_send.at[2], one_recv.at[2], {"view": inner},
        )

    def ratio_edge():
        return remote(
            ratios.at[:, :, ys(chunks, 1)], ratios.at[:, :, ys(last, 1, parity=1 - odd)],
            one_send.at[3], one_recv.at[3], {"view": inner},
        )

    def start_near(c):
        for p in range(pieces):
            near_halo(c, p).start()

    def start_rec(c):
        for k in range(1, views):
            rec(k, c).start()

    own_rows = pl.ds(pl.multiple_of(view * quarter, quarter), quarter)
    own_copy = pltpu.make_async_copy(
        recorded_hbm.at[0, :, own_rows], recorded.at[view], own_sem
    )
    ins = [
        pltpu.make_async_copy(src, dst, in_sem.at[i])
        for i, (src, dst) in enumerate((
            (estimate_hbm, estimate), (psf_hbm, psf_ref), (assign_hbm, assign_ref),
            (half_hbm, half_ref), (flags_hbm, flags_ref),
        ))
    ]
    for copy in ins:
        copy.start()
    barrier = pltpu.get_barrier_semaphore()
    for k in range(1, views):
        pl.semaphore_signal(barrier, inc=1, device_id={"view": peer(k)}, device_id_type=MESH)
    pl.semaphore_signal(barrier, inc=1, device_id={"tile": partner}, device_id_type=MESH)

    @pl.when(has_far)
    def _():
        pl.semaphore_signal(barrier, inc=1, device_id={"tile": far_tile}, device_id_type=MESH)

    @pl.when(has_next)
    def _():
        pl.semaphore_signal(barrier, inc=1, device_id={"tile": next_tile}, device_id_type=MESH)

    own_copy.start()
    ins[0].wait()
    rounded[:, CHUNK:CHUNK + quarter, :] = estimate[...].astype(BF16)
    pl.semaphore_wait(
        barrier, views + has_far.astype(jnp.int32) + has_next.astype(jnp.int32)
    )

    @pl.when(has_outer)
    def _():
        first_edge().start()

    start_near(1)
    start_near(2)
    for c in range(1, chunks + 1):
        start_rec(c)

    @pl.when(jnp.logical_not(has_far))
    def _():
        around[side] = jnp.zeros(around.shape[1:], BF16)

    @pl.when(jnp.logical_not(has_next))
    def _():
        far_in[...] = jnp.zeros_like(far_in)

    spare = pl.ds(pl.multiple_of(odd * (last + 1) * CHUNK, CHUNK), 2 * CHUNK)
    ratios[:, :, spare, :] = jnp.zeros((views, slab, 2 * CHUNK, depth), BF16)

    @pl.when(jnp.logical_not(has_outer))
    def _():
        mixed[:, :, ys(0), :] = jnp.zeros((views, slab, CHUNK, depth), BF16)

    taps[...] = jnp.zeros_like(taps)
    for copy in ins[1:]:
        copy.wait()
    rows, cols = slab * GROUP, 3 * slab * GROUP
    tap = lax.broadcasted_iota(jnp.int32, (taps.shape[1], cols), 0)
    spot = lax.broadcasted_iota(jnp.int32, (taps.shape[1], cols), 1)
    spread = ((spot == GROUP * (tap + slab - HALF)) & (tap < TAPS)).astype(F32).astype(BF16)
    tap = lax.broadcasted_iota(jnp.int32, (taps.shape[1], taps.shape[1]), 0)
    spot = lax.broadcasted_iota(jnp.int32, (taps.shape[1], taps.shape[1]), 1)
    mirror = ((spot == TAPS - 1 - tap) & (tap < TAPS)).astype(F32).astype(BF16)
    low_rows = pl.ds(pl.multiple_of(2 * rows * side, rows), rows)
    high_rows = pl.ds(pl.multiple_of(2 * rows * (1 - side), rows), rows)
    for s in range(views):
        lines = picked_taps(assign_ref[s], half_ref, psf_ref, taps)
        line = dot(lines.astype(BF16), spread)[0:1]
        block = pltpu.roll(jnp.broadcast_to(line, (rows, cols)), 0, 1, stride=1, stride_axis=0)
        wide_a[s * rows:(s + 1) * rows, :] = block.astype(BF16)
        turned = block.T.astype(BF16)
        wide_b[low_rows, s * rows:(s + 1) * rows] = turned[:rows]
        wide_b[rows:2 * rows, s * rows:(s + 1) * rows] = turned[rows:2 * rows]
        wide_b[high_rows, s * rows:(s + 1) * rows] = turned[2 * rows:]
        cy[s] = stacked_band(lines[1:2])
        cyt[s] = stacked_band(dot(lines.astype(BF16), mirror)[1:2])
        across = band(lines[2:3], depth)
        cz[s] = across.astype(BF16)
        czt[s] = across.T.astype(BF16)
        totals = jnp.sum(lines, axis=1, keepdims=True)
        scale = 1.0 / (totals[0:1] * totals[1:2] * totals[2:3])
        scales[s:s + 1, :] = jnp.broadcast_to(scale, (1, depth))

    @pl.when(has_outer)
    def _():
        first_edge().wait_recv()
        start_near(0)

    for c in range(3, chunks + 1):
        start_near(c)

    def early(c):
        return c + (c < 2).astype(jnp.int32) - 2 * (c == 2).astype(jnp.int32)

    def pass_on(c):
        for p in range(pieces):
            near_halo(c, p).wait_recv()

            @pl.when(has_next)
            def _():
                far_halo(c, p).start()

    def blur_x(c):
        @pl.when(has_far)
        def _():
            for p in range(pieces):
                far_halo(c, p).wait_recv()

        cells = jnp.concatenate(
            [around[0, :, ys(c), :], rounded[:, ys(c), :], around[1, :, ys(c), :]], axis=0
        ).astype(F32)
        blurs = []
        for h in range(0, CHUNK, GROUP):
            some = cells[:, h:h + GROUP, :].reshape(cols, depth).astype(BF16)
            blurs.append(dot(wide_a[...], some).reshape(views * slab, GROUP, depth))
        mixed[:, :, ys(c), :] = (
            jnp.concatenate(blurs, axis=1).astype(BF16).reshape(views, slab, CHUNK, depth)
        )

        @pl.when(c == chunks)
        def _():
            mix_edge().start()

    def along_y(ref, bands, s, c, base):
        parts = []
        for g in range(0, slab, STACK):
            data = ref[s, g:g + STACK, ys(c, base, 3 * CHUNK), :]
            parts.append(dot(bands[s], data.reshape(3 * CHUNK * STACK, depth)).astype(BF16))
        return jnp.concatenate(parts, axis=0)

    def divide(c):
        @pl.when(c == 1)
        def _():
            own_copy.wait()

        @pl.when(c == chunks)
        def _():
            mix_edge().wait_recv()

        for k in range(1, views):
            rec(k, c).wait_recv()

        for s in range(views):
            blurred = dot(along_y(mixed, cy, s, c, -1), czt[s]) * scales[s:s + 1, :]
            seen = recorded[s, :, ys(c, -1), :].astype(F32).reshape(slab * CHUNK, depth)
            ratio = (seen / blurred).astype(BF16)
            ratios[s, :, ys(c, 1), :] = ratio.reshape(slab, CHUNK, depth)

        @pl.when(c == chunks)
        def _():
            ratio_edge().start()

    def packed(block, target, *at):
        mean = (jnp.sum(block, axis=1) * (1.0 / CHUNK)).astype(BF16)
        target[(slice(0, slab), *at)] = (block - mean.astype(F32)[:, None, :]).astype(BF16)
        target[(slab, *at)] = mean

    def unpacked(source, *at):
        mean = source[(slab, *at)].astype(F32)[:, None, :]
        return source[(slice(0, slab), *at)].astype(F32) + mean

    def back(c):
        @pl.when(c == chunks)
        def _():
            ratio_edge().wait_recv()

        halves = [[] for _ in range(0, CHUNK, GROUP)]
        for s in range(views):
            across = dot(along_y(ratios, cyt, s, c, 0), cz[s]) * scales[s:s + 1, :]
            across = across.reshape(slab, CHUNK, depth)
            for h, half in enumerate(halves):
                some = across[:, h * GROUP:(h + 1) * GROUP, :]
                half.append(some.reshape(rows, depth).astype(BF16))
        blurs = []
        for half in halves:
            some = jnp.concatenate(half, axis=0)
            blurs.append(dot(wide_b[...], some).reshape(3 * slab, GROUP, depth))
        wide = jnp.concatenate(blurs, axis=1)
        for p in range(pieces):
            packed(wide[:slab, :, zs(p)], far_out, ys(c), zs(p))

            @pl.when(has_far)
            def _():
                far_sum(c, p).start()

        center[:, ys(c), :] = wide[slab:2 * slab]
        beside[:, ys(c), :] = wide[2 * slab:]

    def combine(c):
        for p in range(pieces):
            @pl.when(has_next)
            def _():
                far_sum(c, p).wait_recv()

            came = unpacked(far_in, ys(c), zs(p))
            packed(beside[:, ys(c), zs(p)] + came, near_out, ys(c), zs(p))
            near_sum(c, p).start()

    def finish(c):
        for p in range(pieces):
            near_sum(c, p).wait_recv()
        center[:, ys(c), :] += unpacked(near_in, ys(c), slice(None))

        @pl.when(c == 0)
        def _():
            packed(center[:, ys(0), :], edge_out, slice(0, CHUNK), slice(None))
            last_edge().start()

        @pl.when((c == 1) & has_outer)
        def _():
            last_edge().wait_recv()
            center[:, ys(1), :] += unpacked(edge_in, slice(0, CHUNK), slice(None))

        @pl.when(c > 0)
        def _():
            spot = place(c, odd)
            for i in range(0, slab, GROUP):
                for h in range(CHUNK // GROUP):
                    near = pl.ds(pl.multiple_of(spot * CHUNK + h * GROUP, GROUP), GROUP)
                    here = pl.ds(pl.multiple_of((spot - 1) * CHUNK + h * GROUP, GROUP), GROUP)
                    flag = flags_ref[i // GROUP, (spot - 1) * (CHUNK // GROUP) + h]
                    was = estimate[i:i + GROUP, here, :]
                    now = was * (center[i:i + GROUP, near, :] * (1.0 / views))
                    out[i:i + GROUP, here, :] = jnp.where(flag > 0, now, was)

    def step(j, carry):
        def at(first, count, body, order=lambda c: c):
            c = order(j - first)

            @pl.when((j >= first) & (j < first + count) & active(c))
            def _():
                body(c)

        at(0, chunks + 1, pass_on, early)
        at(1, chunks + 1, blur_x, early)
        at(3, chunks, divide, lambda c: c + 1)
        at(3, chunks + 1, back)
        at(4, chunks + 1, combine)
        at(6, chunks + 1, finish)
        return carry

    lax.fori_loop(0, chunks + 7, step, 0)

    def wait_sends(c, carry):
        @pl.when(active(c))
        def _():
            for p in range(pieces):
                near_halo(c, p).wait_send()
                near_sum(c, p).wait_send()

            @pl.when(has_next)
            def _():
                for p in range(pieces):
                    far_halo(c, p).wait_send()

            @pl.when(has_far)
            def _():
                for p in range(pieces):
                    far_sum(c, p).wait_send()

        @pl.when(c > 0)
        def _():
            for k in range(1, views):
                rec(k, c).wait_send()

        return carry

    lax.fori_loop(0, chunks + 1, wait_sends, 0)

    @pl.when(has_outer)
    def _():
        first_edge().wait_send()
        last_edge().wait_send()

    mix_edge().wait_send()
    ratio_edge().wait_send()


def shards(recorded, estimate, psf_taps, half_width, assign, flags):
    views = lax.axis_size("view")
    slab, quarter, depth = estimate.shape
    chunks = quarter // CHUNK
    rows, cols = slab * GROUP, 3 * slab * GROUP
    hbm = pl.BlockSpec(memory_space=pltpu.HBM)
    half_width, psf_taps = half_width.T, psf_taps.transpose(1, 0, 2)
    dma = pltpu.SemaphoreType.DMA
    reach = quarter + 2 * CHUNK
    sums = pltpu.VMEM((slab + 1, reach, depth), BF16)
    edge = pltpu.VMEM((slab + 1, CHUNK, depth), BF16)
    total = pltpu.VMEM((slab, reach, depth), F32)
    each = dma((depth // LANES, chunks + 1))
    return pl.pallas_call(
        kernel,
        out_shape=jax.ShapeDtypeStruct(estimate.shape, F32),
        in_specs=[hbm] * 6,
        out_specs=pl.BlockSpec(memory_space=pltpu.VMEM),
        scratch_shapes=[
            pltpu.SMEM(assign.shape, assign.dtype),
            pltpu.SMEM(half_width.shape, half_width.dtype),
            pltpu.SMEM(flags.shape, flags.dtype),
            pltpu.VMEM(psf_taps.shape, F32),
            pltpu.VMEM(estimate.shape, F32),
            pltpu.VMEM((slab, reach, depth), BF16),
            pltpu.VMEM((8, 256), F32),
            pltpu.VMEM((8, depth), F32),
            pltpu.VMEM((views * rows, cols), BF16),
            pltpu.VMEM((cols, views * rows), BF16),
            pltpu.VMEM((views, STACK * CHUNK, 3 * STACK * CHUNK), BF16),
            pltpu.VMEM((views, STACK * CHUNK, 3 * STACK * CHUNK), BF16),
            pltpu.VMEM((views, depth, depth), BF16),
            pltpu.VMEM((views, depth, depth), BF16),
            pltpu.VMEM((views, slab, quarter, depth), BF16),
            pltpu.VMEM((2, slab, reach, depth), BF16),
            pltpu.VMEM((views, slab, reach, depth), BF16),
            pltpu.VMEM((views, slab, reach + 2 * CHUNK, depth), BF16),
            total, total,
            sums, sums, sums, sums, edge, edge,
            dma((5,)), dma,
            dma((views - 1, chunks)), dma((views - 1, chunks)),
            each, each, each, each, each, each, each, each,
            dma((4,)), dma((4,)),
        ],
        compiler_params=pltpu.CompilerParams(
            collective_id=0, has_side_effects=True, vmem_limit_bytes=VMEM_LIMIT
        ),
        name="deconvolve",
    )(*(
        pltpu.with_memory_space_constraint(a, pltpu.HBM)
        for a in (assign, half_width, flags, psf_taps, estimate, recorded)
    ))


def solution(mesh):
    placed = (
        P("view", "tile", None, None),
        P("tile", "view", None),
        P(),
        P(),
        P(),
        P("tile", "view"),
    )
    return jax.shard_map(
        shards, mesh=mesh, in_specs=placed, out_specs=P("tile", "view", None), check_vma=False
    )
```

```python
import jax
import jax.numpy as jnp
from jax import lax
from jax.experimental import pallas as pl
from jax.experimental.pallas import tpu as pltpu
from jax.sharding import PartitionSpec as P

TAPS = 31
HALF = TAPS // 2
GROUP = 8
CHUNK = 16
STACK = 2
LANES = 128
VMEM_LIMIT = 40 << 20
F32 = jnp.float32
BF16 = jnp.bfloat16
MESH = pl.DeviceIdType.MESH


def dot(a, b):
    return jnp.dot(a, b, preferred_element_type=F32)


def picked_taps(entry, half_ref, psf_ref, taps):
    for d in range(3):
        taps[d:d + 1, 0:TAPS] = psf_ref[d, pl.ds(entry, 1), :]
    row = lax.broadcasted_iota(jnp.int32, taps.shape, 0)
    col = lax.broadcasted_iota(jnp.int32, taps.shape, 1)
    width = jnp.where(
        row == 0, half_ref[0, entry], jnp.where(row == 1, half_ref[1, entry], half_ref[2, entry])
    )
    keep = (jnp.abs(col - HALF) <= width) & (col < TAPS) & (row < 3)
    return jnp.where(keep, taps[...], 0.0).astype(BF16).astype(F32)


def band(line, size):
    rolled = pltpu.roll(
        jnp.broadcast_to(line, (size, size)), size - HALF, 1, stride=1, stride_axis=0
    )
    row = lax.broadcasted_iota(jnp.int32, (size, size), 0)
    col = lax.broadcasted_iota(jnp.int32, (size, size), 1)
    return jnp.where(jnp.abs(row - col) <= HALF, rolled, 0.0)


def stacked_band(line):
    width = line.shape[1]
    blocks = [
        pltpu.roll(
            jnp.broadcast_to(line, (CHUNK, width)), 3 * CHUNK * i + CHUNK - HALF, 1,
            stride=1, stride_axis=0,
        )
        for i in range(STACK)
    ]
    return jnp.concatenate(blocks, axis=0)[:, :3 * CHUNK * STACK].astype(BF16)


def kernel(
    assign_hbm, half_hbm, flags_hbm, psf_hbm, estimate_hbm, recorded_hbm, out,
    assign_ref, half_ref, flags_ref, psf_ref, estimate,
    rounded, taps, scales, wide_a, wide_b, cy, cyt, cz, czt, recorded,
    around, mixed, ratios, center, beside,
    far_out, far_in, near_out, near_in, edge_out, edge_in,
    in_sem, own_sem, rec_send, rec_recv, near_send, near_recv, pass_send, pass_recv,
    far_send, far_recv, pair_send, pair_recv, one_send, one_recv,
):
    slab, quarter, depth = estimate.shape
    views = recorded.shape[0]
    chunks = quarter // CHUNK
    pieces = depth // LANES
    tile, view = lax.axis_index("tile"), lax.axis_index("view")
    tiles = lax.axis_size("tile")
    side = lax.rem(tile, 2)
    partner = tile + 1 - 2 * side
    far_tile = tile - 2 + 4 * side
    next_tile = tile + 2 - 4 * side
    has_far = (far_tile >= 0) & (far_tile < tiles)
    has_next = (next_tile >= 0) & (next_tile < tiles)
    odd = lax.rem(view, 2)
    inner = view + 1 - 2 * odd
    outer = view - 1 + 2 * odd
    has_outer = (outer >= 0) & (outer < views)
    last = chunks + 1

    def place(c, parity):
        return c + parity * (last - 2 * c)

    def ys(c, base=0, size=CHUNK, parity=odd):
        return pl.ds(pl.multiple_of((place(c, parity) + base) * CHUNK, CHUNK), size)

    def peer(k):
        return lax.rem(view + k, views)

    def active(c):
        return (c > 0) | has_outer

    def remote(src, dst, send, recv, device):
        return pltpu.make_async_remote_copy(
            src_ref=src, dst_ref=dst, send_sem=send, recv_sem=recv,
            device_id=device, device_id_type=MESH,
        )

    def zs(p):
        return slice(p * LANES, (p + 1) * LANES)

    def near_halo(c, p):
        return remote(
            rounded.at[:, ys(c), zs(p)], around.at[side, :, ys(c), zs(p)],
            near_send.at[p, c], near_recv.at[p, c], {"tile": partner},
        )

    def far_halo(c, p):
        return remote(
            around.at[1 - side, :, ys(c), zs(p)], around.at[side, :, ys(c), zs(p)],
            pass_send.at[p, c], pass_recv.at[p, c], {"tile": next_tile},
        )

    def far_sum(c, p):
        return remote(
            far_out.at[:, ys(c), zs(p)], far_in.at[:, ys(c), zs(p)],
            far_send.at[p, c], far_recv.at[p, c], {"tile": far_tile},
        )

    def near_sum(c, p):
        return remote(
            near_out.at[:, ys(c), zs(p)], near_in.at[:, ys(c), zs(p)],
            pair_send.at[p, c], pair_recv.at[p, c], {"tile": partner},
        )

    def rec(k, c):
        to = peer(k)
        parity = lax.rem(to, 2)
        spot = (place(c, parity) - 1) * CHUNK
        return remote(
            recorded_hbm.at[0, :, pl.ds(pl.multiple_of(to * quarter + spot, CHUNK), CHUNK)],
            recorded.at[view, :, pl.ds(pl.multiple_of(spot, CHUNK), CHUNK)],
            rec_send.at[k - 1, c - 1], rec_recv.at[k - 1, c - 1], {"view": to},
        )

    def first_edge():
        return remote(
            rounded.at[:, ys(1)], rounded.at[:, ys(0, parity=1 - odd)],
            one_send.at[0], one_recv.at[0], {"view": outer},
        )

    def last_edge():
        return remote(edge_out, edge_in, one_send.at[1], one_recv.at[1], {"view": outer})

    def mix_edge():
        return remote(
            mixed.at[:, :, ys(chunks)], mixed.at[:, :, ys(last, parity=1 - odd)],
            one_send.at[2], one_recv.at[2], {"view": inner},
        )

    def ratio_edge():
        return remote(
            ratios.at[:, :, ys(chunks, 1)], ratios.at[:, :, ys(last, 1, parity=1 - odd)],
            one_send.at[3], one_recv.at[3], {"view": inner},
        )

    def start_near(c):
        for p in range(pieces):
            near_halo(c, p).start()

    def start_rec(c):
        for k in range(1, views):
            rec(k, c).start()

    own_rows = pl.ds(pl.multiple_of(view * quarter, quarter), quarter)
    own_copy = pltpu.make_async_copy(
        recorded_hbm.at[0, :, own_rows], recorded.at[view], own_sem
    )
    ins = [
        pltpu.make_async_copy(src, dst, in_sem.at[i])
        for i, (src, dst) in enumerate((
            (estimate_hbm, estimate), (psf_hbm, psf_ref), (assign_hbm, assign_ref),
            (half_hbm, half_ref), (flags_hbm, flags_ref),
        ))
    ]
    for copy in ins:
        copy.start()
    barrier = pltpu.get_barrier_semaphore()
    for k in range(1, views):
        pl.semaphore_signal(barrier, inc=1, device_id={"view": peer(k)}, device_id_type=MESH)
    pl.semaphore_signal(barrier, inc=1, device_id={"tile": partner}, device_id_type=MESH)

    @pl.when(has_far)
    def _():
        pl.semaphore_signal(barrier, inc=1, device_id={"tile": far_tile}, device_id_type=MESH)

    @pl.when(has_next)
    def _():
        pl.semaphore_signal(barrier, inc=1, device_id={"tile": next_tile}, device_id_type=MESH)

    own_copy.start()
    ins[0].wait()
    rounded[:, CHUNK:CHUNK + quarter, :] = estimate[...].astype(BF16)
    pl.semaphore_wait(
        barrier, views + has_far.astype(jnp.int32) + has_next.astype(jnp.int32)
    )

    @pl.when(has_outer)
    def _():
        first_edge().start()

    start_near(1)
    start_near(2)
    for c in range(1, chunks + 1):
        start_rec(c)

    @pl.when(jnp.logical_not(has_far))
    def _():
        around[side] = jnp.zeros(around.shape[1:], BF16)

    @pl.when(jnp.logical_not(has_next))
    def _():
        far_in[...] = jnp.zeros_like(far_in)

    spare = pl.ds(pl.multiple_of(odd * (last + 1) * CHUNK, CHUNK), 2 * CHUNK)
    ratios[:, :, spare, :] = jnp.zeros((views, slab, 2 * CHUNK, depth), BF16)

    @pl.when(jnp.logical_not(has_outer))
    def _():
        mixed[:, :, ys(0), :] = jnp.zeros((views, slab, CHUNK, depth), BF16)

    taps[...] = jnp.zeros_like(taps)
    for copy in ins[1:]:
        copy.wait()
    rows, cols = slab * GROUP, 3 * slab * GROUP
    tap = lax.broadcasted_iota(jnp.int32, (taps.shape[1], cols), 0)
    spot = lax.broadcasted_iota(jnp.int32, (taps.shape[1], cols), 1)
    spread = ((spot == GROUP * (tap + slab - HALF)) & (tap < TAPS)).astype(F32).astype(BF16)
    tap = lax.broadcasted_iota(jnp.int32, (taps.shape[1], taps.shape[1]), 0)
    spot = lax.broadcasted_iota(jnp.int32, (taps.shape[1], taps.shape[1]), 1)
    mirror = ((spot == TAPS - 1 - tap) & (tap < TAPS)).astype(F32).astype(BF16)
    low_rows = pl.ds(pl.multiple_of(2 * rows * side, rows), rows)
    high_rows = pl.ds(pl.multiple_of(2 * rows * (1 - side), rows), rows)
    for s in range(views):
        lines = picked_taps(assign_ref[s], half_ref, psf_ref, taps)
        line = dot(lines.astype(BF16), spread)[0:1]
        block = pltpu.roll(jnp.broadcast_to(line, (rows, cols)), 0, 1, stride=1, stride_axis=0)
        wide_a[s * rows:(s + 1) * rows, :] = block.astype(BF16)
        turned = block.T.astype(BF16)
        wide_b[low_rows, s * rows:(s + 1) * rows] = turned[:rows]
        wide_b[rows:2 * rows, s * rows:(s + 1) * rows] = turned[rows:2 * rows]
        wide_b[high_rows, s * rows:(s + 1) * rows] = turned[2 * rows:]
        cy[s] = stacked_band(lines[1:2])
        cyt[s] = stacked_band(dot(lines.astype(BF16), mirror)[1:2])
        across = band(lines[2:3], depth)
        cz[s] = across.astype(BF16)
        czt[s] = across.T.astype(BF16)
        totals = jnp.sum(lines, axis=1, keepdims=True)
        scale = 1.0 / (totals[0:1] * totals[1:2] * totals[2:3])
        scales[s:s + 1, :] = jnp.broadcast_to(scale, (1, depth))

    @pl.when(has_outer)
    def _():
        first_edge().wait_recv()
        start_near(0)

    for c in range(3, chunks + 1):
        start_near(c)

    def early(c):
        return c + (c < 2).astype(jnp.int32) - 2 * (c == 2).astype(jnp.int32)

    def pass_on(c):
        for p in range(pieces):
            near_halo(c, p).wait_recv()

            @pl.when(has_next)
            def _():
                far_halo(c, p).start()

    def blur_x(c):
        @pl.when(has_far)
        def _():
            for p in range(pieces):
                far_halo(c, p).wait_recv()

        cells = jnp.concatenate(
            [around[0, :, ys(c), :], rounded[:, ys(c), :], around[1, :, ys(c), :]], axis=0
        ).astype(F32)
        blurs = []
        for h in range(0, CHUNK, GROUP):
            some = cells[:, h:h + GROUP, :].reshape(cols, depth).astype(BF16)
            blurs.append(dot(wide_a[...], some).reshape(views * slab, GROUP, depth))
        mixed[:, :, ys(c), :] = (
            jnp.concatenate(blurs, axis=1).astype(BF16).reshape(views, slab, CHUNK, depth)
        )

        @pl.when(c == chunks)
        def _():
            mix_edge().start()

    def along_y(ref, bands, s, c, base):
        parts = []
        for g in range(0, slab, STACK):
            data = ref[s, g:g + STACK, ys(c, base, 3 * CHUNK), :]
            parts.append(dot(bands[s], data.reshape(3 * CHUNK * STACK, depth)).astype(BF16))
        return jnp.concatenate(parts, axis=0)

    def divide(c):
        @pl.when(c == 1)
        def _():
            own_copy.wait()

        @pl.when(c == chunks)
        def _():
            mix_edge().wait_recv()

        for k in range(1, views):
            rec(k, c).wait_recv()

        lines = [along_y(mixed, cy, s, c, -1) for s in range(views)]
        blurs = [dot(line, czt[s]) for s, line in enumerate(lines)]
        for s in range(views):
            blurred = blurs[s] * scales[s:s + 1, :]
            seen = recorded[s, :, ys(c, -1), :].astype(F32).reshape(slab * CHUNK, depth)
            ratio = (seen / blurred).astype(BF16)
            ratios[s, :, ys(c, 1), :] = ratio.reshape(slab, CHUNK, depth)

        @pl.when(c == chunks)
        def _():
            ratio_edge().start()

    def packed(block, target, *at):
        mean = (jnp.sum(block, axis=1) * (1.0 / CHUNK)).astype(BF16)
        target[(slice(0, slab), *at)] = (block - mean.astype(F32)[:, None, :]).astype(BF16)
        target[(slab, *at)] = mean

    def unpacked(source, *at):
        mean = source[(slab, *at)].astype(F32)[:, None, :]
        return source[(slice(0, slab), *at)].astype(F32) + mean

    def back(c):
        @pl.when(c == chunks)
        def _():
            ratio_edge().wait_recv()

        halves = [[] for _ in range(0, CHUNK, GROUP)]
        lines = [along_y(ratios, cyt, s, c, 0) for s in range(views)]
        blurs = [dot(line, cz[s]) for s, line in enumerate(lines)]
        for s in range(views):
            across = blurs[s] * scales[s:s + 1, :]
            across = across.reshape(slab, CHUNK, depth)
            for h, half in enumerate(halves):
                some = across[:, h * GROUP:(h + 1) * GROUP, :]
                half.append(some.reshape(rows, depth).astype(BF16))
        blurs = []
        for half in halves:
            some = jnp.concatenate(half, axis=0)
            blurs.append(dot(wide_b[...], some).reshape(3 * slab, GROUP, depth))
        wide = jnp.concatenate(blurs, axis=1)
        for p in range(pieces):
            packed(wide[:slab, :, zs(p)], far_out, ys(c), zs(p))

            @pl.when(has_far)
            def _():
                far_sum(c, p).start()

        center[:, ys(c), :] = wide[slab:2 * slab]
        beside[:, ys(c), :] = wide[2 * slab:]

    def combine(c):
        for p in range(pieces):
            @pl.when(has_next)
            def _():
                far_sum(c, p).wait_recv()

            came = unpacked(far_in, ys(c), zs(p))
            packed(beside[:, ys(c), zs(p)] + came, near_out, ys(c), zs(p))
            near_sum(c, p).start()

    def finish(c):
        for p in range(pieces):
            near_sum(c, p).wait_recv()

        @pl.when((c == 1) & has_outer)
        def _():
            last_edge().wait_recv()
            center[:, ys(1), :] += unpacked(edge_in, slice(0, CHUNK), slice(None))

        total = center[:, ys(c), :] + unpacked(near_in, ys(c), slice(None))

        @pl.when(c == 0)
        def _():
            packed(total, edge_out, slice(0, CHUNK), slice(None))
            last_edge().start()

        @pl.when(c > 0)
        def _():
            spot = place(c, odd) - 1
            for i in range(0, slab, GROUP):
                for h in range(CHUNK // GROUP):
                    here = pl.ds(pl.multiple_of(spot * CHUNK + h * GROUP, GROUP), GROUP)
                    flag = flags_ref[i // GROUP, spot * (CHUNK // GROUP) + h]
                    part = total[i:i + GROUP, h * GROUP:(h + 1) * GROUP, :]
                    was = estimate[i:i + GROUP, here, :]
                    now = was * (part * (1.0 / views))
                    out[i:i + GROUP, here, :] = jnp.where(flag > 0, now, was)

    def step(j, carry):
        def at(first, count, body, order=lambda c: c):
            c = order(j - first)

            @pl.when((j >= first) & (j < first + count) & active(c))
            def _():
                body(c)

        at(0, chunks + 1, pass_on, early)
        at(5, chunks + 1, combine)
        at(1, chunks + 1, blur_x, early)
        at(3, chunks, divide, lambda c: c + 1)
        at(3, chunks + 1, back)
        at(6, chunks + 1, finish)
        return carry

    lax.fori_loop(0, chunks + 7, step, 0)

    def wait_sends(c, carry):
        @pl.when(active(c))
        def _():
            for p in range(pieces):
                near_halo(c, p).wait_send()
                near_sum(c, p).wait_send()

            @pl.when(has_next)
            def _():
                for p in range(pieces):
                    far_halo(c, p).wait_send()

            @pl.when(has_far)
            def _():
                for p in range(pieces):
                    far_sum(c, p).wait_send()

        @pl.when(c > 0)
        def _():
            for k in range(1, views):
                rec(k, c).wait_send()

        return carry

    lax.fori_loop(0, chunks + 1, wait_sends, 0)

    @pl.when(has_outer)
    def _():
        first_edge().wait_send()
        last_edge().wait_send()

    mix_edge().wait_send()
    ratio_edge().wait_send()


def shards(recorded, estimate, psf_taps, half_width, assign, flags):
    views = lax.axis_size("view")
    slab, quarter, depth = estimate.shape
    chunks = quarter // CHUNK
    rows, cols = slab * GROUP, 3 * slab * GROUP
    hbm = pl.BlockSpec(memory_space=pltpu.HBM)
    half_width, psf_taps = half_width.T, psf_taps.transpose(1, 0, 2)
    dma = pltpu.SemaphoreType.DMA
    reach = quarter + 2 * CHUNK
    sums = pltpu.VMEM((slab + 1, reach, depth), BF16)
    edge = pltpu.VMEM((slab + 1, CHUNK, depth), BF16)
    total = pltpu.VMEM((slab, reach, depth), F32)
    each = dma((depth // LANES, chunks + 1))
    return pl.pallas_call(
        kernel,
        out_shape=jax.ShapeDtypeStruct(estimate.shape, F32),
        in_specs=[hbm] * 6,
        out_specs=pl.BlockSpec(memory_space=pltpu.VMEM),
        scratch_shapes=[
            pltpu.SMEM(assign.shape, assign.dtype),
            pltpu.SMEM(half_width.shape, half_width.dtype),
            pltpu.SMEM(flags.shape, flags.dtype),
            pltpu.VMEM(psf_taps.shape, F32),
            pltpu.VMEM(estimate.shape, F32),
            pltpu.VMEM((slab, reach, depth), BF16),
            pltpu.VMEM((8, 256), F32),
            pltpu.VMEM((8, depth), F32),
            pltpu.VMEM((views * rows, cols), BF16),
            pltpu.VMEM((cols, views * rows), BF16),
            pltpu.VMEM((views, STACK * CHUNK, 3 * STACK * CHUNK), BF16),
            pltpu.VMEM((views, STACK * CHUNK, 3 * STACK * CHUNK), BF16),
            pltpu.VMEM((views, depth, depth), BF16),
            pltpu.VMEM((views, depth, depth), BF16),
            pltpu.VMEM((views, slab, quarter, depth), BF16),
            pltpu.VMEM((2, slab, reach, depth), BF16),
            pltpu.VMEM((views, slab, reach, depth), BF16),
            pltpu.VMEM((views, slab, reach + 2 * CHUNK, depth), BF16),
            total, total,
            sums, sums, sums, sums, edge, edge,
            dma((5,)), dma,
            dma((views - 1, chunks)), dma((views - 1, chunks)),
            each, each, each, each, each, each, each, each,
            dma((4,)), dma((4,)),
        ],
        compiler_params=pltpu.CompilerParams(
            collective_id=0, has_side_effects=True, vmem_limit_bytes=VMEM_LIMIT
        ),
        name="deconvolve",
    )(*(
        pltpu.with_memory_space_constraint(a, pltpu.HBM)
        for a in (assign, half_width, flags, psf_taps, estimate, recorded)
    ))


def solution(mesh):
    placed = (
        P("view", "tile", None, None),
        P("tile", "view", None),
        P(),
        P(),
        P(),
        P("tile", "view"),
    )
    return jax.shard_map(
        shards, mesh=mesh, in_specs=placed, out_specs=P("tile", "view", None), check_vma=False
    )
```

```python
import jax
import jax.numpy as jnp
from jax import lax
from jax.experimental import pallas as pl
from jax.experimental.pallas import tpu as pltpu
from jax.sharding import PartitionSpec as P

TAPS = 31
HALF = TAPS // 2
GROUP = 8
CHUNK = 16
STACK = 2
LANES = 128
VMEM_LIMIT = 40 << 20
F32 = jnp.float32
BF16 = jnp.bfloat16
MESH = pl.DeviceIdType.MESH


def dot(a, b):
    return jnp.dot(a, b, preferred_element_type=F32)


def picked_taps(entry, half_ref, psf_ref, taps):
    for d in range(3):
        taps[d:d + 1, 0:TAPS] = psf_ref[d, pl.ds(entry, 1), :]
    row = lax.broadcasted_iota(jnp.int32, taps.shape, 0)
    col = lax.broadcasted_iota(jnp.int32, taps.shape, 1)
    width = jnp.where(
        row == 0, half_ref[0, entry], jnp.where(row == 1, half_ref[1, entry], half_ref[2, entry])
    )
    keep = (jnp.abs(col - HALF) <= width) & (col < TAPS) & (row < 3)
    return jnp.where(keep, taps[...], 0.0).astype(BF16).astype(F32)


def band(line, size):
    rolled = pltpu.roll(
        jnp.broadcast_to(line, (size, size)), size - HALF, 1, stride=1, stride_axis=0
    )
    row = lax.broadcasted_iota(jnp.int32, (size, size), 0)
    col = lax.broadcasted_iota(jnp.int32, (size, size), 1)
    return jnp.where(jnp.abs(row - col) <= HALF, rolled, 0.0)


def stacked_band(line):
    width = line.shape[1]
    blocks = [
        pltpu.roll(
            jnp.broadcast_to(line, (CHUNK, width)), 3 * CHUNK * i + CHUNK - HALF, 1,
            stride=1, stride_axis=0,
        )
        for i in range(STACK)
    ]
    return jnp.concatenate(blocks, axis=0)[:, :3 * CHUNK * STACK].astype(BF16)


def kernel(
    assign_hbm, half_hbm, flags_hbm, psf_hbm, estimate_hbm, recorded_hbm, out,
    assign_ref, half_ref, flags_ref, psf_ref, estimate,
    rounded, taps, scales, wide_a, wide_b, cy, cyt, cz, czt, recorded,
    around, mixed, ratios, center, beside,
    far_out, far_in, near_out, near_in, edge_out, edge_in,
    in_sem, own_sem, rec_send, rec_recv, near_send, near_recv, pass_send, pass_recv,
    far_send, far_recv, pair_send, pair_recv, one_send, one_recv,
):
    slab, quarter, depth = estimate.shape
    views = recorded.shape[0]
    chunks = quarter // CHUNK
    pieces = depth // LANES
    tile, view = lax.axis_index("tile"), lax.axis_index("view")
    tiles = lax.axis_size("tile")
    side = lax.rem(tile, 2)
    partner = tile + 1 - 2 * side
    far_tile = tile - 2 + 4 * side
    next_tile = tile + 2 - 4 * side
    has_far = (far_tile >= 0) & (far_tile < tiles)
    has_next = (next_tile >= 0) & (next_tile < tiles)
    odd = lax.rem(view, 2)
    inner = view + 1 - 2 * odd
    outer = view - 1 + 2 * odd
    has_outer = (outer >= 0) & (outer < views)
    last = chunks + 1

    def place(c, parity):
        return c + parity * (last - 2 * c)

    def ys(c, base=0, size=CHUNK, parity=odd):
        return pl.ds(pl.multiple_of((place(c, parity) + base) * CHUNK, CHUNK), size)

    def peer(k):
        return lax.rem(view + k, views)

    def active(c):
        return (c > 0) | has_outer

    def remote(src, dst, send, recv, device):
        return pltpu.make_async_remote_copy(
            src_ref=src, dst_ref=dst, send_sem=send, recv_sem=recv,
            device_id=device, device_id_type=MESH,
        )

    def zs(p):
        return slice(p * LANES, (p + 1) * LANES)

    def near_halo(c, p):
        return remote(
            rounded.at[:, ys(c), zs(p)], around.at[side, :, ys(c), zs(p)],
            near_send.at[p, c], near_recv.at[p, c], {"tile": partner},
        )

    reach = pl.ds(1 - side, HALF)
    spare = side * (slab - 1)

    def far_halo(c, p):
        return remote(
            around.at[1 - side, reach, ys(c), zs(p)], around.at[side, reach, ys(c), zs(p)],
            pass_send.at[p, c], pass_recv.at[p, c], {"tile": next_tile},
        )

    def far_sum(c, p):
        return remote(
            far_out.at[:, ys(c), zs(p)], far_in.at[:, ys(c), zs(p)],
            far_send.at[p, c], far_recv.at[p, c], {"tile": far_tile},
        )

    def near_sum(c, p):
        return remote(
            near_out.at[:, ys(c), zs(p)], near_in.at[:, ys(c), zs(p)],
            pair_send.at[p, c], pair_recv.at[p, c], {"tile": partner},
        )

    def rec(k, c):
        to = peer(k)
        parity = lax.rem(to, 2)
        spot = (place(c, parity) - 1) * CHUNK
        return remote(
            recorded_hbm.at[0, :, pl.ds(pl.multiple_of(to * quarter + spot, CHUNK), CHUNK)],
            recorded.at[view, :, pl.ds(pl.multiple_of(spot, CHUNK), CHUNK)],
            rec_send.at[k - 1, c - 1], rec_recv.at[k - 1, c - 1], {"view": to},
        )

    def first_edge():
        return remote(
            rounded.at[:, ys(1)], rounded.at[:, ys(0, parity=1 - odd)],
            one_send.at[0], one_recv.at[0], {"view": outer},
        )

    def last_edge():
        return remote(edge_out, edge_in, one_send.at[1], one_recv.at[1], {"view": outer})

    def mix_edge():
        return remote(
            mixed.at[:, :, ys(chunks)], mixed.at[:, :, ys(last, parity=1 - odd)],
            one_send.at[2], one_recv.at[2], {"view": inner},
        )

    def ratio_edge():
        return remote(
            ratios.at[:, :, ys(chunks, 1)], ratios.at[:, :, ys(last, 1, parity=1 - odd)],
            one_send.at[3], one_recv.at[3], {"view": inner},
        )

    def start_near(c):
        for p in range(pieces):
            near_halo(c, p).start()

    def start_rec(c):
        for k in range(1, views):
            rec(k, c).start()

    own_rows = pl.ds(pl.multiple_of(view * quarter, quarter), quarter)
    own_copy = pltpu.make_async_copy(
        recorded_hbm.at[0, :, own_rows], recorded.at[view], own_sem
    )
    ins = [
        pltpu.make_async_copy(src, dst, in_sem.at[i])
        for i, (src, dst) in enumerate((
            (estimate_hbm, estimate), (psf_hbm, psf_ref), (assign_hbm, assign_ref),
            (half_hbm, half_ref), (flags_hbm, flags_ref),
        ))
    ]
    for copy in ins:
        copy.start()
    barrier = pltpu.get_barrier_semaphore()
    for k in range(1, views):
        pl.semaphore_signal(barrier, inc=1, device_id={"view": peer(k)}, device_id_type=MESH)
    pl.semaphore_signal(barrier, inc=1, device_id={"tile": partner}, device_id_type=MESH)

    @pl.when(has_far)
    def _():
        pl.semaphore_signal(barrier, inc=1, device_id={"tile": far_tile}, device_id_type=MESH)

    @pl.when(has_next)
    def _():
        pl.semaphore_signal(barrier, inc=1, device_id={"tile": next_tile}, device_id_type=MESH)

    own_copy.start()
    ins[0].wait()
    rounded[:, CHUNK:CHUNK + quarter, :] = estimate[...].astype(BF16)
    pl.semaphore_wait(
        barrier, views + has_far.astype(jnp.int32) + has_next.astype(jnp.int32)
    )

    start_near(1)

    @pl.when(has_outer)
    def _():
        first_edge().start()

    start_near(2)
    for c in range(1, chunks + 1):
        start_rec(c)

    @pl.when(jnp.logical_not(has_far))
    def _():
        around[side] = jnp.zeros(around.shape[1:], BF16)

    @pl.when(jnp.logical_not(has_next))
    def _():
        far_in[...] = jnp.zeros_like(far_in)

    around[side, spare] = jnp.zeros(around.shape[2:], BF16)
    beyond = pl.ds(pl.multiple_of(odd * (last + 1) * CHUNK, CHUNK), 2 * CHUNK)
    ratios[:, :, beyond, :] = jnp.zeros((views, slab, 2 * CHUNK, depth), BF16)

    @pl.when(jnp.logical_not(has_outer))
    def _():
        mixed[:, :, ys(0), :] = jnp.zeros((views, slab, CHUNK, depth), BF16)

    taps[...] = jnp.zeros_like(taps)
    for copy in ins[1:]:
        copy.wait()
    rows, cols = slab * GROUP, 3 * slab * GROUP
    tap = lax.broadcasted_iota(jnp.int32, (taps.shape[1], cols), 0)
    spot = lax.broadcasted_iota(jnp.int32, (taps.shape[1], cols), 1)
    spread = ((spot == GROUP * (tap + slab - HALF)) & (tap < TAPS)).astype(F32).astype(BF16)
    tap = lax.broadcasted_iota(jnp.int32, (taps.shape[1], taps.shape[1]), 0)
    spot = lax.broadcasted_iota(jnp.int32, (taps.shape[1], taps.shape[1]), 1)
    mirror = ((spot == TAPS - 1 - tap) & (tap < TAPS)).astype(F32).astype(BF16)
    low_rows = pl.ds(pl.multiple_of(2 * rows * side, rows), rows)
    high_rows = pl.ds(pl.multiple_of(2 * rows * (1 - side), rows), rows)
    for s in range(views):
        lines = picked_taps(assign_ref[s], half_ref, psf_ref, taps)
        line = dot(lines.astype(BF16), spread)[0:1]
        block = pltpu.roll(jnp.broadcast_to(line, (rows, cols)), 0, 1, stride=1, stride_axis=0)
        wide_a[s * rows:(s + 1) * rows, :] = block.astype(BF16)
        turned = block.T.astype(BF16)
        wide_b[low_rows, s * rows:(s + 1) * rows] = turned[:rows]
        wide_b[rows:2 * rows, s * rows:(s + 1) * rows] = turned[rows:2 * rows]
        wide_b[high_rows, s * rows:(s + 1) * rows] = turned[2 * rows:]
        cy[s] = stacked_band(lines[1:2])
        cyt[s] = stacked_band(dot(lines.astype(BF16), mirror)[1:2])
        across = band(lines[2:3], depth)
        cz[s] = across.astype(BF16)
        czt[s] = across.T.astype(BF16)
        totals = jnp.sum(lines, axis=1, keepdims=True)
        scale = 1.0 / (totals[0:1] * totals[1:2] * totals[2:3])
        scales[s:s + 1, :] = jnp.broadcast_to(scale, (1, depth))

    @pl.when(has_outer)
    def _():
        first_edge().wait_recv()
        start_near(0)

    for c in range(3, chunks + 1):
        start_near(c)

    def early(c):
        return c + (c < 2).astype(jnp.int32) - 2 * (c == 2).astype(jnp.int32)

    def pass_on(c):
        for p in range(pieces):
            near_halo(c, p).wait_recv()

            @pl.when(has_next)
            def _():
                far_halo(c, p).start()

    def blur_x(c):
        @pl.when(has_far)
        def _():
            for p in range(pieces):
                far_halo(c, p).wait_recv()

        cells = jnp.concatenate(
            [around[0, :, ys(c), :], rounded[:, ys(c), :], around[1, :, ys(c), :]], axis=0
        ).astype(F32)
        blurs = []
        for h in range(0, CHUNK, GROUP):
            some = cells[:, h:h + GROUP, :].reshape(cols, depth).astype(BF16)
            blurs.append(dot(wide_a[...], some).reshape(views * slab, GROUP, depth))
        mixed[:, :, ys(c), :] = (
            jnp.concatenate(blurs, axis=1).astype(BF16).reshape(views, slab, CHUNK, depth)
        )

        @pl.when(c == chunks)
        def _():
            mix_edge().start()

    def along_y(ref, bands, s, c, base):
        parts = []
        for g in range(0, slab, STACK):
            data = ref[s, g:g + STACK, ys(c, base, 3 * CHUNK), :]
            parts.append(dot(bands[s], data.reshape(3 * CHUNK * STACK, depth)).astype(BF16))
        return jnp.concatenate(parts, axis=0)

    def divide(c):
        @pl.when(c == 1)
        def _():
            own_copy.wait()

        @pl.when(c == chunks)
        def _():
            mix_edge().wait_recv()

        lines = [along_y(mixed, cy, s, c, -1) for s in range(views)]
        blurs = [dot(line, czt[s]) * scales[s:s + 1, :] for s, line in enumerate(lines)]
        for k in range(1, views):
            rec(k, c).wait_recv()

        for s in range(views):
            blurred = blurs[s]
            seen = recorded[s, :, ys(c, -1), :].astype(F32).reshape(slab * CHUNK, depth)
            ratio = (seen / blurred).astype(BF16)
            ratios[s, :, ys(c, 1), :] = ratio.reshape(slab, CHUNK, depth)

        @pl.when(c == chunks)
        def _():
            ratio_edge().start()

    def packed(block, target, *at, layer=slab):
        mean = (jnp.sum(block, axis=1) * (1.0 / CHUNK)).astype(BF16)
        target[(slice(0, slab), *at)] = (block - mean.astype(F32)[:, None, :]).astype(BF16)
        target[(layer, *at)] = mean

    def unpacked(source, *at, layer=slab):
        mean = source[(layer, *at)].astype(F32)[:, None, :]
        return source[(slice(0, slab), *at)].astype(F32) + mean

    def back(c):
        @pl.when(c == chunks)
        def _():
            ratio_edge().wait_recv()

        halves = [[] for _ in range(0, CHUNK, GROUP)]
        lines = [along_y(ratios, cyt, s, c, 0) for s in range(views)]
        blurs = [dot(line, cz[s]) for s, line in enumerate(lines)]
        for s in range(views):
            across = blurs[s] * scales[s:s + 1, :]
            across = across.reshape(slab, CHUNK, depth)
            for h, half in enumerate(halves):
                some = across[:, h * GROUP:(h + 1) * GROUP, :]
                half.append(some.reshape(rows, depth).astype(BF16))
        blurs = []
        for half in halves:
            some = jnp.concatenate(half, axis=0)
            blurs.append(dot(wide_b[...], some).reshape(3 * slab, GROUP, depth))
        wide = jnp.concatenate(blurs, axis=1)
        for p in range(pieces):
            packed(wide[:slab, :, zs(p)], far_out, ys(c), zs(p), layer=spare)

            @pl.when(has_far)
            def _():
                far_sum(c, p).start()

        center[:, ys(c), :] = wide[slab:2 * slab]
        beside[:, ys(c), :] = wide[2 * slab:]

    def combine(c):
        for p in range(pieces):
            @pl.when(has_next)
            def _():
                far_sum(c, p).wait_recv()

            came = unpacked(far_in, ys(c), zs(p), layer=spare)
            came = jnp.concatenate(
                [came[:1] * side.astype(F32), came[1:slab - 1],
                 came[slab - 1:] * (1 - side).astype(F32)], axis=0
            )
            packed(beside[:, ys(c), zs(p)] + came, near_out, ys(c), zs(p))
            near_sum(c, p).start()

    def finish(c):
        for p in range(pieces):
            near_sum(c, p).wait_recv()

        @pl.when((c == 1) & has_outer)
        def _():
            last_edge().wait_recv()
            center[:, ys(1), :] += unpacked(edge_in, slice(0, CHUNK), slice(None))

        total = center[:, ys(c), :] + unpacked(near_in, ys(c), slice(None))

        @pl.when(c == 0)
        def _():
            packed(total, edge_out, slice(0, CHUNK), slice(None))
            last_edge().start()

        @pl.when(c > 0)
        def _():
            spot = place(c, odd) - 1
            for i in range(0, slab, GROUP):
                for h in range(CHUNK // GROUP):
                    here = pl.ds(pl.multiple_of(spot * CHUNK + h * GROUP, GROUP), GROUP)
                    flag = flags_ref[i // GROUP, spot * (CHUNK // GROUP) + h]
                    part = total[i:i + GROUP, h * GROUP:(h + 1) * GROUP, :]
                    was = estimate[i:i + GROUP, here, :]
                    now = was * (part * (1.0 / views))
                    out[i:i + GROUP, here, :] = jnp.where(flag > 0, now, was)

    def step(j, carry):
        def at(first, count, body, order=lambda c: c):
            c = order(j - first)

            @pl.when((j >= first) & (j < first + count) & active(c))
            def _():
                body(c)

        at(0, chunks + 1, pass_on, early)
        at(5, chunks + 1, combine)
        at(1, chunks + 1, blur_x, early)
        at(3, chunks, divide, lambda c: c + 1)
        at(3, chunks + 1, back)
        at(6, chunks + 1, finish)
        return carry

    lax.fori_loop(0, chunks + 7, step, 0)

    def wait_sends(c, carry):
        @pl.when(active(c))
        def _():
            for p in range(pieces):
                near_halo(c, p).wait_send()
                near_sum(c, p).wait_send()

            @pl.when(has_next)
            def _():
                for p in range(pieces):
                    far_halo(c, p).wait_send()

            @pl.when(has_far)
            def _():
                for p in range(pieces):
                    far_sum(c, p).wait_send()

        @pl.when(c > 0)
        def _():
            for k in range(1, views):
                rec(k, c).wait_send()

        return carry

    lax.fori_loop(0, chunks + 1, wait_sends, 0)

    @pl.when(has_outer)
    def _():
        first_edge().wait_send()
        last_edge().wait_send()

    mix_edge().wait_send()
    ratio_edge().wait_send()


def shards(recorded, estimate, psf_taps, half_width, assign, flags):
    views = lax.axis_size("view")
    slab, quarter, depth = estimate.shape
    chunks = quarter // CHUNK
    rows, cols = slab * GROUP, 3 * slab * GROUP
    hbm = pl.BlockSpec(memory_space=pltpu.HBM)
    half_width, psf_taps = half_width.T, psf_taps.transpose(1, 0, 2)
    dma = pltpu.SemaphoreType.DMA
    reach = quarter + 2 * CHUNK
    sums = pltpu.VMEM((slab + 1, reach, depth), BF16)
    faces = pltpu.VMEM((slab, reach, depth), BF16)
    edge = pltpu.VMEM((slab + 1, CHUNK, depth), BF16)
    total = pltpu.VMEM((slab, reach, depth), F32)
    each = dma((depth // LANES, chunks + 1))
    return pl.pallas_call(
        kernel,
        out_shape=jax.ShapeDtypeStruct(estimate.shape, F32),
        in_specs=[hbm] * 6,
        out_specs=pl.BlockSpec(memory_space=pltpu.VMEM),
        scratch_shapes=[
            pltpu.SMEM(assign.shape, assign.dtype),
            pltpu.SMEM(half_width.shape, half_width.dtype),
            pltpu.SMEM(flags.shape, flags.dtype),
            pltpu.VMEM(psf_taps.shape, F32),
            pltpu.VMEM(estimate.shape, F32),
            pltpu.VMEM((slab, reach, depth), BF16),
            pltpu.VMEM((8, 256), F32),
            pltpu.VMEM((8, depth), F32),
            pltpu.VMEM((views * rows, cols), BF16),
            pltpu.VMEM((cols, views * rows), BF16),
            pltpu.VMEM((views, STACK * CHUNK, 3 * STACK * CHUNK), BF16),
            pltpu.VMEM((views, STACK * CHUNK, 3 * STACK * CHUNK), BF16),
            pltpu.VMEM((views, depth, depth), BF16),
            pltpu.VMEM((views, depth, depth), BF16),
            pltpu.VMEM((views, slab, quarter, depth), BF16),
            pltpu.VMEM((2, slab, reach, depth), BF16),
            pltpu.VMEM((views, slab, reach, depth), BF16),
            pltpu.VMEM((views, slab, reach + 2 * CHUNK, depth), BF16),
            total, total,
            faces, faces, sums, sums, edge, edge,
            dma((5,)), dma,
            dma((views - 1, chunks)), dma((views - 1, chunks)),
            each, each, each, each, each, each, each, each,
            dma((4,)), dma((4,)),
        ],
        compiler_params=pltpu.CompilerParams(
            collective_id=0, has_side_effects=True, vmem_limit_bytes=VMEM_LIMIT
        ),
        name="deconvolve",
    )(*(
        pltpu.with_memory_space_constraint(a, pltpu.HBM)
        for a in (assign, half_width, flags, psf_taps, estimate, recorded)
    ))


def solution(mesh):
    placed = (
        P("view", "tile", None, None),
        P("tile", "view", None),
        P(),
        P(),
        P(),
        P("tile", "view"),
    )
    return jax.shard_map(
        shards, mesh=mesh, in_specs=placed, out_specs=P("tile", "view", None), check_vma=False
    )
```

```python
import jax
import jax.numpy as jnp
from jax import lax
from jax.experimental import pallas as pl
from jax.experimental.pallas import tpu as pltpu
from jax.sharding import PartitionSpec as P

TAPS = 31
HALF = TAPS // 2
GROUP = 8
CHUNK = 16
STACK = 2
LANES = 128
VMEM_LIMIT = 40 << 20
F32 = jnp.float32
BF16 = jnp.bfloat16
MESH = pl.DeviceIdType.MESH


def dot(a, b):
    return jnp.dot(a, b, preferred_element_type=F32)


def picked_taps(entry, half_ref, psf_ref, taps):
    for d in range(3):
        taps[d:d + 1, 0:TAPS] = psf_ref[d, pl.ds(entry, 1), :]
    row = lax.broadcasted_iota(jnp.int32, taps.shape, 0)
    col = lax.broadcasted_iota(jnp.int32, taps.shape, 1)
    width = jnp.where(
        row == 0, half_ref[0, entry], jnp.where(row == 1, half_ref[1, entry], half_ref[2, entry])
    )
    keep = (jnp.abs(col - HALF) <= width) & (col < TAPS) & (row < 3)
    return jnp.where(keep, taps[...], 0.0).astype(BF16).astype(F32)


def band(line, size):
    rolled = pltpu.roll(
        jnp.broadcast_to(line, (size, size)), size - HALF, 1, stride=1, stride_axis=0
    )
    row = lax.broadcasted_iota(jnp.int32, (size, size), 0)
    col = lax.broadcasted_iota(jnp.int32, (size, size), 1)
    return jnp.where(jnp.abs(row - col) <= HALF, rolled, 0.0)


def stacked_band(line):
    width = line.shape[1]
    blocks = [
        pltpu.roll(
            jnp.broadcast_to(line, (CHUNK, width)), 3 * CHUNK * i + CHUNK - HALF, 1,
            stride=1, stride_axis=0,
        )
        for i in range(STACK)
    ]
    return jnp.concatenate(blocks, axis=0)[:, :3 * CHUNK * STACK].astype(BF16)


def kernel(
    assign_hbm, half_hbm, flags_hbm, psf_hbm, estimate_hbm, recorded_hbm, out,
    assign_ref, half_ref, flags_ref, psf_ref, estimate,
    rounded, taps, scales, wide_a, wide_b, cy, cyt, cz, czt, recorded,
    around, mixed, ratios, center, beside,
    far_out, far_in, near_out, near_in, edge_out, edge_in,
    in_sem, own_sem, rec_send, rec_recv, near_send, near_recv, pass_send, pass_recv,
    far_send, far_recv, pair_send, pair_recv, one_send, one_recv,
):
    slab, quarter, depth = estimate.shape
    views = recorded.shape[0]
    chunks = quarter // CHUNK
    pieces = depth // LANES
    tile, view = lax.axis_index("tile"), lax.axis_index("view")
    tiles = lax.axis_size("tile")
    side = lax.rem(tile, 2)
    partner = tile + 1 - 2 * side
    far_tile = tile - 2 + 4 * side
    next_tile = tile + 2 - 4 * side
    has_far = (far_tile >= 0) & (far_tile < tiles)
    has_next = (next_tile >= 0) & (next_tile < tiles)
    odd = lax.rem(view, 2)
    inner = view + 1 - 2 * odd
    outer = view - 1 + 2 * odd
    has_outer = (outer >= 0) & (outer < views)
    last = chunks + 1

    def place(c, parity):
        return c + parity * (last - 2 * c)

    def ys(c, base=0, size=CHUNK, parity=odd):
        return pl.ds(pl.multiple_of((place(c, parity) + base) * CHUNK, CHUNK), size)

    def peer(k):
        return lax.rem(view + k, views)

    def active(c):
        return (c > 0) | has_outer

    def remote(src, dst, send, recv, device):
        return pltpu.make_async_remote_copy(
            src_ref=src, dst_ref=dst, send_sem=send, recv_sem=recv,
            device_id=device, device_id_type=MESH,
        )

    def zs(p):
        return slice(p * LANES, (p + 1) * LANES)

    def near_halo(c, p):
        return remote(
            rounded.at[:, ys(c), zs(p)], around.at[side, :, ys(c), zs(p)],
            near_send.at[p, c], near_recv.at[p, c], {"tile": partner},
        )

    reach = pl.ds(1 - side, HALF)
    spare = side * (slab - 1)

    def far_halo(c, p):
        return remote(
            around.at[1 - side, reach, ys(c), zs(p)], around.at[side, reach, ys(c), zs(p)],
            pass_send.at[p, c], pass_recv.at[p, c], {"tile": next_tile},
        )

    def far_sum(c, p):
        return remote(
            far_out.at[:, ys(c), zs(p)], far_in.at[:, ys(c), zs(p)],
            far_send.at[p, c], far_recv.at[p, c], {"tile": far_tile},
        )

    def near_sum(c, p):
        return remote(
            near_out.at[:, ys(c), zs(p)], near_in.at[:, ys(c), zs(p)],
            pair_send.at[p, c], pair_recv.at[p, c], {"tile": partner},
        )

    def rec(k, c):
        to = peer(k)
        parity = lax.rem(to, 2)
        spot = (place(c, parity) - 1) * CHUNK
        return remote(
            recorded_hbm.at[0, :, pl.ds(pl.multiple_of(to * quarter + spot, CHUNK), CHUNK)],
            recorded.at[view, :, pl.ds(pl.multiple_of(spot, CHUNK), CHUNK)],
            rec_send.at[k - 1, c - 1], rec_recv.at[k - 1, c - 1], {"view": to},
        )

    def first_edge():
        return remote(
            rounded.at[:, ys(1)], rounded.at[:, ys(0, parity=1 - odd)],
            one_send.at[0], one_recv.at[0], {"view": outer},
        )

    def last_edge():
        return remote(edge_out, edge_in, one_send.at[1], one_recv.at[1], {"view": outer})

    def mix_edge():
        return remote(
            mixed.at[:, :, ys(chunks)], mixed.at[:, :, ys(last, parity=1 - odd)],
            one_send.at[2], one_recv.at[2], {"view": inner},
        )

    def ratio_edge():
        return remote(
            ratios.at[:, :, ys(chunks, 1)], ratios.at[:, :, ys(last, 1, parity=1 - odd)],
            one_send.at[3], one_recv.at[3], {"view": inner},
        )

    def start_near(c):
        for p in range(pieces):
            near_halo(c, p).start()

    def start_rec(c):
        for k in range(1, views):
            rec(k, c).start()

    own_rows = pl.ds(pl.multiple_of(view * quarter, quarter), quarter)
    own_copy = pltpu.make_async_copy(
        recorded_hbm.at[0, :, own_rows], recorded.at[view], own_sem
    )
    ins = [
        pltpu.make_async_copy(src, dst, in_sem.at[i])
        for i, (src, dst) in enumerate((
            (estimate_hbm, estimate), (psf_hbm, psf_ref), (assign_hbm, assign_ref),
            (half_hbm, half_ref), (flags_hbm, flags_ref),
        ))
    ]
    for copy in ins:
        copy.start()
    barrier = pltpu.get_barrier_semaphore()
    for k in range(1, views):
        pl.semaphore_signal(barrier, inc=1, device_id={"view": peer(k)}, device_id_type=MESH)
    pl.semaphore_signal(barrier, inc=1, device_id={"tile": partner}, device_id_type=MESH)

    @pl.when(has_far)
    def _():
        pl.semaphore_signal(barrier, inc=1, device_id={"tile": far_tile}, device_id_type=MESH)

    @pl.when(has_next)
    def _():
        pl.semaphore_signal(barrier, inc=1, device_id={"tile": next_tile}, device_id_type=MESH)

    own_copy.start()
    ins[0].wait()
    rounded[:, CHUNK:CHUNK + quarter, :] = estimate[...].astype(BF16)
    pl.semaphore_wait(
        barrier, views + has_far.astype(jnp.int32) + has_next.astype(jnp.int32)
    )

    start_near(1)

    @pl.when(has_outer)
    def _():
        first_edge().start()

    start_near(2)
    for c in range(1, chunks + 1):
        start_rec(c)

    @pl.when(jnp.logical_not(has_far))
    def _():
        around[side] = jnp.zeros(around.shape[1:], BF16)

    @pl.when(jnp.logical_not(has_next))
    def _():
        far_in[...] = jnp.zeros_like(far_in)

    around[side, spare] = jnp.zeros(around.shape[2:], BF16)
    beyond = pl.ds(pl.multiple_of(odd * (last + 1) * CHUNK, CHUNK), 2 * CHUNK)
    ratios[:, :, beyond, :] = jnp.zeros((views, slab, 2 * CHUNK, depth), BF16)

    @pl.when(jnp.logical_not(has_outer))
    def _():
        mixed[:, :, ys(0), :] = jnp.zeros((views, slab, CHUNK, depth), BF16)

    taps[...] = jnp.zeros_like(taps)
    for copy in ins[1:]:
        copy.wait()
    rows, cols = slab * GROUP, 3 * slab * GROUP
    tap = lax.broadcasted_iota(jnp.int32, (taps.shape[1], cols), 0)
    spot = lax.broadcasted_iota(jnp.int32, (taps.shape[1], cols), 1)
    spread = ((spot == GROUP * (tap + slab - HALF)) & (tap < TAPS)).astype(F32).astype(BF16)
    tap = lax.broadcasted_iota(jnp.int32, (taps.shape[1], taps.shape[1]), 0)
    spot = lax.broadcasted_iota(jnp.int32, (taps.shape[1], taps.shape[1]), 1)
    mirror = ((spot == TAPS - 1 - tap) & (tap < TAPS)).astype(F32).astype(BF16)
    low_rows = pl.ds(pl.multiple_of(2 * rows * side, rows), rows)
    high_rows = pl.ds(pl.multiple_of(2 * rows * (1 - side), rows), rows)
    for s in range(views):
        lines = picked_taps(assign_ref[s], half_ref, psf_ref, taps)
        line = dot(lines.astype(BF16), spread)[0:1]
        block = pltpu.roll(jnp.broadcast_to(line, (rows, cols)), 0, 1, stride=1, stride_axis=0)
        wide_a[s * rows:(s + 1) * rows, :] = block.astype(BF16)
        turned = block.T.astype(BF16)
        wide_b[low_rows, s * rows:(s + 1) * rows] = turned[:rows]
        wide_b[rows:2 * rows, s * rows:(s + 1) * rows] = turned[rows:2 * rows]
        wide_b[high_rows, s * rows:(s + 1) * rows] = turned[2 * rows:]
        cy[s] = stacked_band(lines[1:2])
        cyt[s] = stacked_band(dot(lines.astype(BF16), mirror)[1:2])
        across = band(lines[2:3], depth)
        cz[s] = across.astype(BF16)
        czt[s] = across.T.astype(BF16)
        totals = jnp.sum(lines, axis=1, keepdims=True)
        scale = 1.0 / (totals[0:1] * totals[1:2] * totals[2:3])
        scales[s:s + 1, :] = jnp.broadcast_to(scale, (1, depth))

    @pl.when(has_outer)
    def _():
        first_edge().wait_recv()
        start_near(0)

    for c in range(3, chunks + 1):
        start_near(c)

    def early(c):
        return c + (c < 2).astype(jnp.int32) - 2 * (c == 2).astype(jnp.int32)

    def pass_on(c):
        for p in range(pieces):
            near_halo(c, p).wait_recv()

            @pl.when(has_next)
            def _():
                far_halo(c, p).start()

    def blur_x(c):
        @pl.when(has_far)
        def _():
            for p in range(pieces):
                far_halo(c, p).wait_recv()

        cells = jnp.concatenate(
            [around[0, :, ys(c), :], rounded[:, ys(c), :], around[1, :, ys(c), :]], axis=0
        ).astype(F32)
        blurs = []
        for h in range(0, CHUNK, GROUP):
            some = cells[:, h:h + GROUP, :].reshape(cols, depth).astype(BF16)
            blurs.append(dot(wide_a[...], some).reshape(views * slab, GROUP, depth))
        mixed[:, :, ys(c), :] = (
            jnp.concatenate(blurs, axis=1).astype(BF16).reshape(views, slab, CHUNK, depth)
        )

        @pl.when(c == chunks)
        def _():
            mix_edge().start()

    def along_y(ref, bands, s, c, base):
        parts = []
        for g in range(0, slab, STACK):
            data = ref[s, g:g + STACK, ys(c, base, 3 * CHUNK), :]
            parts.append(dot(bands[s], data.reshape(3 * CHUNK * STACK, depth)).astype(BF16))
        return jnp.concatenate(parts, axis=0)

    def divide(c):
        @pl.when(c == 1)
        def _():
            own_copy.wait()

        @pl.when(c == chunks)
        def _():
            mix_edge().wait_recv()

        lines = [along_y(mixed, cy, s, c, -1) for s in range(views)]
        blurs = [dot(line, czt[s]) * scales[s:s + 1, :] for s, line in enumerate(lines)]
        for k in range(1, views):
            rec(k, c).wait_recv()

        for s in range(views):
            blurred = blurs[s]
            seen = recorded[s, :, ys(c, -1), :].astype(F32).reshape(slab * CHUNK, depth)
            ratio = (seen / blurred).astype(BF16)
            ratios[s, :, ys(c, 1), :] = ratio.reshape(slab, CHUNK, depth)

        @pl.when(c == chunks)
        def _():
            ratio_edge().start()

    def packed(block, target, *at, layer=slab):
        mean = (jnp.sum(block, axis=1) * (1.0 / CHUNK)).astype(BF16)
        target[(slice(0, slab), *at)] = (block - mean.astype(F32)[:, None, :]).astype(BF16)
        target[(layer, *at)] = mean

    def unpacked(source, *at, layer=slab):
        mean = source[(layer, *at)].astype(F32)[:, None, :]
        return source[(slice(0, slab), *at)].astype(F32) + mean

    def back(c):
        @pl.when(c == chunks)
        def _():
            ratio_edge().wait_recv()

        halves = [[] for _ in range(0, CHUNK, GROUP)]
        lines = [along_y(ratios, cyt, s, c, 0) for s in range(views)]
        blurs = [dot(line, cz[s]) for s, line in enumerate(lines)]
        for s in range(views):
            across = blurs[s] * scales[s:s + 1, :]
            across = across.reshape(slab, CHUNK, depth)
            for h, half in enumerate(halves):
                some = across[:, h * GROUP:(h + 1) * GROUP, :]
                half.append(some.reshape(rows, depth).astype(BF16))
        blurs = []
        for half in halves:
            some = jnp.concatenate(half, axis=0)
            blurs.append(dot(wide_b[...], some).reshape(3 * slab, GROUP, depth))
        wide = jnp.concatenate(blurs, axis=1)
        for p in range(pieces):
            packed(wide[:slab, :, zs(p)], far_out, ys(c), zs(p), layer=spare)

            @pl.when(has_far)
            def _():
                far_sum(c, p).start()

        center[:, ys(c), :] = wide[slab:2 * slab]
        beside[:, ys(c), :] = wide[2 * slab:]

    def combine(c):
        for p in range(pieces):
            @pl.when(has_next)
            def _():
                far_sum(c, p).wait_recv()

            came = unpacked(far_in, ys(c), zs(p), layer=spare)
            came = jnp.concatenate(
                [came[:1] * side.astype(F32), came[1:slab - 1],
                 came[slab - 1:] * (1 - side).astype(F32)], axis=0
            )
            packed(beside[:, ys(c), zs(p)] + came, near_out, ys(c), zs(p))
            near_sum(c, p).start()

    def finish(c):
        for p in range(pieces):
            near_sum(c, p).wait_recv()

        @pl.when((c == 1) & has_outer)
        def _():
            last_edge().wait_recv()
            center[:, ys(1), :] += unpacked(edge_in, slice(0, CHUNK), slice(None))

        total = center[:, ys(c), :] + unpacked(near_in, ys(c), slice(None))

        @pl.when(c == 0)
        def _():
            packed(total, edge_out, slice(0, CHUNK), slice(None))
            last_edge().start()

        @pl.when(c > 0)
        def _():
            spot = place(c, odd) - 1
            for i in range(0, slab, GROUP):
                for h in range(CHUNK // GROUP):
                    here = pl.ds(pl.multiple_of(spot * CHUNK + h * GROUP, GROUP), GROUP)
                    flag = flags_ref[i // GROUP, spot * (CHUNK // GROUP) + h]
                    part = total[i:i + GROUP, h * GROUP:(h + 1) * GROUP, :]
                    was = estimate[i:i + GROUP, here, :]
                    now = was * (part * (1.0 / views))
                    out[i:i + GROUP, here, :] = jnp.where(flag > 0, now, was)

    def step(j, carry):
        def at(first, count, body, order=lambda c: c):
            c = order(j - first)

            @pl.when((j >= first) & (j < first + count) & active(c))
            def _():
                body(c)

        at(0, chunks + 1, pass_on, early)
        at(1, chunks + 1, blur_x, early)
        at(5, chunks + 1, combine)
        at(3, chunks, divide, lambda c: c + 1)
        at(3, chunks + 1, back)
        at(6, chunks + 1, finish)
        return carry

    lax.fori_loop(0, chunks + 7, step, 0)

    def wait_sends(c, carry):
        @pl.when(active(c))
        def _():
            for p in range(pieces):
                near_halo(c, p).wait_send()
                near_sum(c, p).wait_send()

            @pl.when(has_next)
            def _():
                for p in range(pieces):
                    far_halo(c, p).wait_send()

            @pl.when(has_far)
            def _():
                for p in range(pieces):
                    far_sum(c, p).wait_send()

        @pl.when(c > 0)
        def _():
            for k in range(1, views):
                rec(k, c).wait_send()

        return carry

    lax.fori_loop(0, chunks + 1, wait_sends, 0)

    @pl.when(has_outer)
    def _():
        first_edge().wait_send()
        last_edge().wait_send()

    mix_edge().wait_send()
    ratio_edge().wait_send()


def shards(recorded, estimate, psf_taps, half_width, assign, flags):
    views = lax.axis_size("view")
    slab, quarter, depth = estimate.shape
    chunks = quarter // CHUNK
    rows, cols = slab * GROUP, 3 * slab * GROUP
    hbm = pl.BlockSpec(memory_space=pltpu.HBM)
    half_width, psf_taps = half_width.T, psf_taps.transpose(1, 0, 2)
    dma = pltpu.SemaphoreType.DMA
    reach = quarter + 2 * CHUNK
    sums = pltpu.VMEM((slab + 1, reach, depth), BF16)
    faces = pltpu.VMEM((slab, reach, depth), BF16)
    edge = pltpu.VMEM((slab + 1, CHUNK, depth), BF16)
    total = pltpu.VMEM((slab, reach, depth), F32)
    each = dma((depth // LANES, chunks + 1))
    return pl.pallas_call(
        kernel,
        out_shape=jax.ShapeDtypeStruct(estimate.shape, F32),
        in_specs=[hbm] * 6,
        out_specs=pl.BlockSpec(memory_space=pltpu.VMEM),
        scratch_shapes=[
            pltpu.SMEM(assign.shape, assign.dtype),
            pltpu.SMEM(half_width.shape, half_width.dtype),
            pltpu.SMEM(flags.shape, flags.dtype),
            pltpu.VMEM(psf_taps.shape, F32),
            pltpu.VMEM(estimate.shape, F32),
            pltpu.VMEM((slab, reach, depth), BF16),
            pltpu.VMEM((8, 256), F32),
            pltpu.VMEM((8, depth), F32),
            pltpu.VMEM((views * rows, cols), BF16),
            pltpu.VMEM((cols, views * rows), BF16),
            pltpu.VMEM((views, STACK * CHUNK, 3 * STACK * CHUNK), BF16),
            pltpu.VMEM((views, STACK * CHUNK, 3 * STACK * CHUNK), BF16),
            pltpu.VMEM((views, depth, depth), BF16),
            pltpu.VMEM((views, depth, depth), BF16),
            pltpu.VMEM((views, slab, quarter, depth), BF16),
            pltpu.VMEM((2, slab, reach, depth), BF16),
            pltpu.VMEM((views, slab, reach, depth), BF16),
            pltpu.VMEM((views, slab, reach + 2 * CHUNK, depth), BF16),
            total, total,
            faces, faces, sums, sums, edge, edge,
            dma((5,)), dma,
            dma((views - 1, chunks)), dma((views - 1, chunks)),
            each, each, each, each, each, each, each, each,
            dma((4,)), dma((4,)),
        ],
        compiler_params=pltpu.CompilerParams(
            collective_id=0, has_side_effects=True, vmem_limit_bytes=VMEM_LIMIT
        ),
        name="deconvolve",
    )(*(
        pltpu.with_memory_space_constraint(a, pltpu.HBM)
        for a in (assign, half_width, flags, psf_taps, estimate, recorded)
    ))


def solution(mesh):
    placed = (
        P("view", "tile", None, None),
        P("tile", "view", None),
        P(),
        P(),
        P(),
        P("tile", "view"),
    )
    return jax.shard_map(
        shards, mesh=mesh, in_specs=placed, out_specs=P("tile", "view", None), check_vma=False
    )
```

```python
import jax
import jax.numpy as jnp
from jax import lax
from jax.experimental import pallas as pl
from jax.experimental.pallas import tpu as pltpu
from jax.sharding import PartitionSpec as P

TAPS = 31
HALF = TAPS // 2
GROUP = 8
CHUNK = 16
STACK = 2
LANES = 128
VMEM_LIMIT = 40 << 20
F32 = jnp.float32
BF16 = jnp.bfloat16
MESH = pl.DeviceIdType.MESH


def dot(a, b):
    return jnp.dot(a, b, preferred_element_type=F32)


def picked_taps(entry, half_ref, psf_ref, taps):
    for d in range(3):
        taps[d:d + 1, 0:TAPS] = psf_ref[d, pl.ds(entry, 1), :]
    row = lax.broadcasted_iota(jnp.int32, taps.shape, 0)
    col = lax.broadcasted_iota(jnp.int32, taps.shape, 1)
    width = jnp.where(
        row == 0, half_ref[0, entry], jnp.where(row == 1, half_ref[1, entry], half_ref[2, entry])
    )
    keep = (jnp.abs(col - HALF) <= width) & (col < TAPS) & (row < 3)
    return jnp.where(keep, taps[...], 0.0).astype(BF16).astype(F32)


def band(line, size):
    rolled = pltpu.roll(
        jnp.broadcast_to(line, (size, size)), size - HALF, 1, stride=1, stride_axis=0
    )
    row = lax.broadcasted_iota(jnp.int32, (size, size), 0)
    col = lax.broadcasted_iota(jnp.int32, (size, size), 1)
    return jnp.where(jnp.abs(row - col) <= HALF, rolled, 0.0)


def stacked_band(line):
    width = line.shape[1]
    blocks = [
        pltpu.roll(
            jnp.broadcast_to(line, (CHUNK, width)), 3 * CHUNK * i + CHUNK - HALF, 1,
            stride=1, stride_axis=0,
        )
        for i in range(STACK)
    ]
    return jnp.concatenate(blocks, axis=0)[:, :3 * CHUNK * STACK].astype(BF16)


def kernel(
    assign_hbm, half_hbm, flags_hbm, psf_hbm, estimate_hbm, recorded_hbm, out,
    assign_ref, half_ref, flags_ref, psf_ref, estimate,
    rounded, taps, scales, wide_a, wide_b, cy, cyt, cz, czt, recorded,
    around, mixed, ratios, center, beside,
    far_out, far_in, near_out, near_in, edge_out, edge_in,
    in_sem, own_sem, rec_send, rec_recv, near_send, near_recv, pass_send, pass_recv,
    far_send, far_recv, pair_send, pair_recv, one_send, one_recv, view_send, view_recv,
):
    slab, quarter, depth = estimate.shape
    views = recorded.shape[0]
    chunks = quarter // CHUNK
    pieces = depth // LANES
    tile, view = lax.axis_index("tile"), lax.axis_index("view")
    tiles = lax.axis_size("tile")
    side = lax.rem(tile, 2)
    partner = tile + 1 - 2 * side
    far_tile = tile - 2 + 4 * side
    next_tile = tile + 2 - 4 * side
    has_far = (far_tile >= 0) & (far_tile < tiles)
    has_next = (next_tile >= 0) & (next_tile < tiles)
    odd = lax.rem(view, 2)
    inner = view + 1 - 2 * odd
    outer = view - 1 + 2 * odd
    has_outer = (outer >= 0) & (outer < views)
    last = chunks + 1

    def place(c, parity):
        return c + parity * (last - 2 * c)

    def ys(c, base=0, size=CHUNK, parity=odd):
        return pl.ds(pl.multiple_of((place(c, parity) + base) * CHUNK, CHUNK), size)

    def peer(k):
        return lax.rem(view + k, views)

    def active(c):
        return (c > 0) | has_outer

    def remote(src, dst, send, recv, device):
        return pltpu.make_async_remote_copy(
            src_ref=src, dst_ref=dst, send_sem=send, recv_sem=recv,
            device_id=device, device_id_type=MESH,
        )

    def zs(p):
        return slice(p * LANES, (p + 1) * LANES)

    def near_halo(c, p):
        return remote(
            rounded.at[:, ys(c), zs(p)], around.at[side, :, ys(c), zs(p)],
            near_send.at[p, c], near_recv.at[p, c], {"tile": partner},
        )

    reach = pl.ds(1 - side, HALF)
    spare = side * (slab - 1)

    def far_halo(c, p):
        return remote(
            around.at[1 - side, reach, ys(c), zs(p)], around.at[side, reach, ys(c), zs(p)],
            pass_send.at[p, c], pass_recv.at[p, c], {"tile": next_tile},
        )

    def far_sum(c, p):
        return remote(
            far_out.at[:, ys(c), zs(p)], far_in.at[:, ys(c), zs(p)],
            far_send.at[p, c], far_recv.at[p, c], {"tile": far_tile},
        )

    def near_sum(c, p):
        return remote(
            near_out.at[:, ys(c), zs(p)], near_in.at[:, ys(c), zs(p)],
            pair_send.at[p, c], pair_recv.at[p, c], {"tile": partner},
        )

    def rec(k, c):
        to = peer(k)
        parity = lax.rem(to, 2)
        spot = (place(c, parity) - 1) * CHUNK
        return remote(
            recorded_hbm.at[0, :, pl.ds(pl.multiple_of(to * quarter + spot, CHUNK), CHUNK)],
            recorded.at[view, :, pl.ds(pl.multiple_of(spot, CHUNK), CHUNK)],
            rec_send.at[k - 1, c - 1], rec_recv.at[k - 1, c - 1], {"view": to},
        )

    def first_edge():
        return remote(
            rounded.at[:, ys(1)], rounded.at[:, ys(0, parity=1 - odd)],
            one_send.at[0], one_recv.at[0], {"view": outer},
        )

    def last_edge():
        return remote(edge_out, edge_in, one_send.at[1], one_recv.at[1], {"view": outer})

    def mix_edge():
        return remote(
            mixed.at[:, :, ys(chunks)], mixed.at[:, :, ys(last, parity=1 - odd)],
            one_send.at[2], one_recv.at[2], {"view": inner},
        )

    def ratio_edge(s):
        return remote(
            ratios.at[s, :, ys(chunks, 1)], ratios.at[s, :, ys(last, 1, parity=1 - odd)],
            view_send.at[s], view_recv.at[s], {"view": inner},
        )

    def start_near(c):
        for p in range(pieces):
            near_halo(c, p).start()

    def start_rec(c):
        for k in range(1, views):
            rec(k, c).start()

    own_rows = pl.ds(pl.multiple_of(view * quarter, quarter), quarter)
    own_copy = pltpu.make_async_copy(
        recorded_hbm.at[0, :, own_rows], recorded.at[view], own_sem
    )
    ins = [
        pltpu.make_async_copy(src, dst, in_sem.at[i])
        for i, (src, dst) in enumerate((
            (estimate_hbm, estimate), (psf_hbm, psf_ref), (assign_hbm, assign_ref),
            (half_hbm, half_ref), (flags_hbm, flags_ref),
        ))
    ]
    for copy in ins:
        copy.start()
    barrier = pltpu.get_barrier_semaphore()
    for k in range(1, views):
        pl.semaphore_signal(barrier, inc=1, device_id={"view": peer(k)}, device_id_type=MESH)
    pl.semaphore_signal(barrier, inc=1, device_id={"tile": partner}, device_id_type=MESH)

    @pl.when(has_far)
    def _():
        pl.semaphore_signal(barrier, inc=1, device_id={"tile": far_tile}, device_id_type=MESH)

    @pl.when(has_next)
    def _():
        pl.semaphore_signal(barrier, inc=1, device_id={"tile": next_tile}, device_id_type=MESH)

    own_copy.start()
    ins[0].wait()
    rounded[:, CHUNK:CHUNK + quarter, :] = estimate[...].astype(BF16)
    pl.semaphore_wait(
        barrier, views + has_far.astype(jnp.int32) + has_next.astype(jnp.int32)
    )

    @pl.when(has_outer)
    def _():
        first_edge().start()

    start_near(1)
    start_near(2)
    for c in range(1, chunks + 1):
        start_rec(c)

    @pl.when(jnp.logical_not(has_far))
    def _():
        around[side] = jnp.zeros(around.shape[1:], BF16)

    @pl.when(jnp.logical_not(has_next))
    def _():
        far_in[...] = jnp.zeros_like(far_in)

    around[side, spare] = jnp.zeros(around.shape[2:], BF16)
    beyond = pl.ds(pl.multiple_of(odd * (last + 1) * CHUNK, CHUNK), 2 * CHUNK)
    ratios[:, :, beyond, :] = jnp.zeros((views, slab, 2 * CHUNK, depth), BF16)

    @pl.when(jnp.logical_not(has_outer))
    def _():
        mixed[:, :, ys(0), :] = jnp.zeros((views, slab, CHUNK, depth), BF16)

    taps[...] = jnp.zeros_like(taps)
    for copy in ins[1:]:
        copy.wait()
    rows, cols = slab * GROUP, 3 * slab * GROUP
    tap = lax.broadcasted_iota(jnp.int32, (taps.shape[1], cols), 0)
    spot = lax.broadcasted_iota(jnp.int32, (taps.shape[1], cols), 1)
    spread = ((spot == GROUP * (tap + slab - HALF)) & (tap < TAPS)).astype(F32).astype(BF16)
    tap = lax.broadcasted_iota(jnp.int32, (taps.shape[1], taps.shape[1]), 0)
    spot = lax.broadcasted_iota(jnp.int32, (taps.shape[1], taps.shape[1]), 1)
    mirror = ((spot == TAPS - 1 - tap) & (tap < TAPS)).astype(F32).astype(BF16)
    low_rows = pl.ds(pl.multiple_of(2 * rows * side, rows), rows)
    high_rows = pl.ds(pl.multiple_of(2 * rows * (1 - side), rows), rows)
    for s in range(views):
        lines = picked_taps(assign_ref[s], half_ref, psf_ref, taps)
        line = dot(lines.astype(BF16), spread)[0:1]
        block = pltpu.roll(jnp.broadcast_to(line, (rows, cols)), 0, 1, stride=1, stride_axis=0)
        wide_a[s * rows:(s + 1) * rows, :] = block.astype(BF16)
        turned = block.T.astype(BF16)
        wide_b[low_rows, s * rows:(s + 1) * rows] = turned[:rows]
        wide_b[rows:2 * rows, s * rows:(s + 1) * rows] = turned[rows:2 * rows]
        wide_b[high_rows, s * rows:(s + 1) * rows] = turned[2 * rows:]
        cy[s] = stacked_band(lines[1:2])
        cyt[s] = stacked_band(dot(lines.astype(BF16), mirror)[1:2])
        across = band(lines[2:3], depth)
        cz[s] = across.astype(BF16)
        czt[s] = across.T.astype(BF16)
        totals = jnp.sum(lines, axis=1, keepdims=True)
        scale = 1.0 / (totals[0:1] * totals[1:2] * totals[2:3])
        scales[s:s + 1, :] = jnp.broadcast_to(scale, (1, depth))

    @pl.when(has_outer)
    def _():
        first_edge().wait_recv()
        start_near(0)

    for c in range(3, chunks + 1):
        start_near(c)

    def early(c):
        return c + (c < 2).astype(jnp.int32) - 2 * (c == 2).astype(jnp.int32)

    def pass_on(c):
        for p in range(pieces):
            near_halo(c, p).wait_recv()

            @pl.when(has_next)
            def _():
                far_halo(c, p).start()

    def blur_x(c):
        @pl.when(has_far)
        def _():
            for p in range(pieces):
                far_halo(c, p).wait_recv()

        cells = jnp.concatenate(
            [around[0, :, ys(c), :], rounded[:, ys(c), :], around[1, :, ys(c), :]], axis=0
        ).astype(F32)
        blurs = []
        for h in range(0, CHUNK, GROUP):
            some = cells[:, h:h + GROUP, :].reshape(cols, depth).astype(BF16)
            blurs.append(dot(wide_a[...], some).reshape(views * slab, GROUP, depth))
        mixed[:, :, ys(c), :] = (
            jnp.concatenate(blurs, axis=1).astype(BF16).reshape(views, slab, CHUNK, depth)
        )

        @pl.when(c == chunks)
        def _():
            mix_edge().start()

    def along_y(ref, bands, s, c, base):
        parts = []
        for g in range(0, slab, STACK):
            data = ref[s, g:g + STACK, ys(c, base, 3 * CHUNK), :]
            parts.append(dot(bands[s], data.reshape(3 * CHUNK * STACK, depth)).astype(BF16))
        return jnp.concatenate(parts, axis=0)

    def divide(c):
        @pl.when(c == 1)
        def _():
            own_copy.wait()

        @pl.when(c == chunks)
        def _():
            mix_edge().wait_recv()

        lines = [along_y(mixed, cy, s, c, -1) for s in range(views)]
        blurs = [dot(line, czt[s]) * scales[s:s + 1, :] for s, line in enumerate(lines)]
        for k in range(1, views):
            rec(k, c).wait_recv()

        for s in range(views):
            blurred = blurs[s]
            seen = recorded[s, :, ys(c, -1), :].astype(F32).reshape(slab * CHUNK, depth)
            ratio = (seen / blurred).astype(BF16)
            ratios[s, :, ys(c, 1), :] = ratio.reshape(slab, CHUNK, depth)

        @pl.when(c == chunks)
        def _():
            for s in range(views):
                ratio_edge(s).start()

    def packed(block, target, *at, layer=slab):
        mean = (jnp.sum(block, axis=1) * (1.0 / CHUNK)).astype(BF16)
        target[(slice(0, slab), *at)] = (block - mean.astype(F32)[:, None, :]).astype(BF16)
        target[(layer, *at)] = mean

    def unpacked(source, *at, layer=slab):
        mean = source[(layer, *at)].astype(F32)[:, None, :]
        return source[(slice(0, slab), *at)].astype(F32) + mean

    def back(c):
        @pl.when(c == chunks)
        def _():
            for s in range(views):
                ratio_edge(s).wait_recv()

        halves = [[] for _ in range(0, CHUNK, GROUP)]
        lines = [along_y(ratios, cyt, s, c, 0) for s in range(views)]
        blurs = [dot(line, cz[s]) for s, line in enumerate(lines)]
        for s in range(views):
            across = blurs[s] * scales[s:s + 1, :]
            across = across.reshape(slab, CHUNK, depth)
            for h, half in enumerate(halves):
                some = across[:, h * GROUP:(h + 1) * GROUP, :]
                half.append(some.reshape(rows, depth).astype(BF16))
        blurs = []
        for half in halves:
            some = jnp.concatenate(half, axis=0)
            blurs.append(dot(wide_b[...], some).reshape(3 * slab, GROUP, depth))
        wide = jnp.concatenate(blurs, axis=1)
        for p in range(pieces):
            packed(wide[:slab, :, zs(p)], far_out, ys(c), zs(p), layer=spare)

            @pl.when(has_far)
            def _():
                far_sum(c, p).start()

        center[:, ys(c), :] = wide[slab:2 * slab]
        beside[:, ys(c), :] = wide[2 * slab:]

    def combine(c):
        for p in range(pieces):
            @pl.when(has_next)
            def _():
                far_sum(c, p).wait_recv()

            came = unpacked(far_in, ys(c), zs(p), layer=spare)
            came = jnp.concatenate(
                [came[:1] * side.astype(F32), came[1:slab - 1],
                 came[slab - 1:] * (1 - side).astype(F32)], axis=0
            )
            packed(beside[:, ys(c), zs(p)] + came, near_out, ys(c), zs(p))
            near_sum(c, p).start()

    def finish(c):
        for p in range(pieces):
            near_sum(c, p).wait_recv()

        @pl.when((c == 1) & has_outer)
        def _():
            last_edge().wait_recv()
            center[:, ys(1), :] += unpacked(edge_in, slice(0, CHUNK), slice(None))

        total = center[:, ys(c), :] + unpacked(near_in, ys(c), slice(None))

        @pl.when(c == 0)
        def _():
            packed(total, edge_out, slice(0, CHUNK), slice(None))
            last_edge().start()

        @pl.when(c > 0)
        def _():
            spot = place(c, odd) - 1
            for i in range(0, slab, GROUP):
                for h in range(CHUNK // GROUP):
                    here = pl.ds(pl.multiple_of(spot * CHUNK + h * GROUP, GROUP), GROUP)
                    flag = flags_ref[i // GROUP, spot * (CHUNK // GROUP) + h]
                    part = total[i:i + GROUP, h * GROUP:(h + 1) * GROUP, :]
                    was = estimate[i:i + GROUP, here, :]
                    now = was * (part * (1.0 / views))
                    out[i:i + GROUP, here, :] = jnp.where(flag > 0, now, was)

    def step(j, carry):
        def at(first, count, body, order=lambda c: c):
            c = order(j - first)

            @pl.when((j >= first) & (j < first + count) & active(c))
            def _():
                body(c)

        at(0, chunks + 1, pass_on, early)
        at(5, chunks + 1, combine)
        at(1, chunks + 1, blur_x, early)
        at(3, chunks, divide, lambda c: c + 1)
        at(3, chunks + 1, back)
        at(6, chunks + 1, finish)
        return carry

    lax.fori_loop(0, chunks + 7, step, 0)

    def wait_sends(c, carry):
        @pl.when(active(c))
        def _():
            for p in range(pieces):
                near_halo(c, p).wait_send()
                near_sum(c, p).wait_send()

            @pl.when(has_next)
            def _():
                for p in range(pieces):
                    far_halo(c, p).wait_send()

            @pl.when(has_far)
            def _():
                for p in range(pieces):
                    far_sum(c, p).wait_send()

        @pl.when(c > 0)
        def _():
            for k in range(1, views):
                rec(k, c).wait_send()

        return carry

    lax.fori_loop(0, chunks + 1, wait_sends, 0)

    @pl.when(has_outer)
    def _():
        first_edge().wait_send()
        last_edge().wait_send()

    mix_edge().wait_send()
    for s in range(views):
        ratio_edge(s).wait_send()


def shards(recorded, estimate, psf_taps, half_width, assign, flags):
    views = lax.axis_size("view")
    slab, quarter, depth = estimate.shape
    chunks = quarter // CHUNK
    rows, cols = slab * GROUP, 3 * slab * GROUP
    hbm = pl.BlockSpec(memory_space=pltpu.HBM)
    half_width, psf_taps = half_width.T, psf_taps.transpose(1, 0, 2)
    dma = pltpu.SemaphoreType.DMA
    reach = quarter + 2 * CHUNK
    sums = pltpu.VMEM((slab + 1, reach, depth), BF16)
    faces = pltpu.VMEM((slab, reach, depth), BF16)
    edge = pltpu.VMEM((slab + 1, CHUNK, depth), BF16)
    total = pltpu.VMEM((slab, reach, depth), F32)
    each = dma((depth // LANES, chunks + 1))
    return pl.pallas_call(
        kernel,
        out_shape=jax.ShapeDtypeStruct(estimate.shape, F32),
        in_specs=[hbm] * 6,
        out_specs=pl.BlockSpec(memory_space=pltpu.VMEM),
        scratch_shapes=[
            pltpu.SMEM(assign.shape, assign.dtype),
            pltpu.SMEM(half_width.shape, half_width.dtype),
            pltpu.SMEM(flags.shape, flags.dtype),
            pltpu.VMEM(psf_taps.shape, F32),
            pltpu.VMEM(estimate.shape, F32),
            pltpu.VMEM((slab, reach, depth), BF16),
            pltpu.VMEM((8, 256), F32),
            pltpu.VMEM((8, depth), F32),
            pltpu.VMEM((views * rows, cols), BF16),
            pltpu.VMEM((cols, views * rows), BF16),
            pltpu.VMEM((views, STACK * CHUNK, 3 * STACK * CHUNK), BF16),
            pltpu.VMEM((views, STACK * CHUNK, 3 * STACK * CHUNK), BF16),
            pltpu.VMEM((views, depth, depth), BF16),
            pltpu.VMEM((views, depth, depth), BF16),
            pltpu.VMEM((views, slab, quarter, depth), BF16),
            pltpu.VMEM((2, slab, reach, depth), BF16),
            pltpu.VMEM((views, slab, reach, depth), BF16),
            pltpu.VMEM((views, slab, reach + 2 * CHUNK, depth), BF16),
            total, total,
            faces, faces, sums, sums, edge, edge,
            dma((5,)), dma,
            dma((views - 1, chunks)), dma((views - 1, chunks)),
            each, each, each, each, each, each, each, each,
            dma((4,)), dma((4,)), dma((views,)), dma((views,)),
        ],
        compiler_params=pltpu.CompilerParams(
            collective_id=0, has_side_effects=True, vmem_limit_bytes=VMEM_LIMIT
        ),
        name="deconvolve",
    )(*(
        pltpu.with_memory_space_constraint(a, pltpu.HBM)
        for a in (assign, half_width, flags, psf_taps, estimate, recorded)
    ))


def solution(mesh):
    placed = (
        P("view", "tile", None, None),
        P("tile", "view", None),
        P(),
        P(),
        P(),
        P("tile", "view"),
    )
    return jax.shard_map(
        shards, mesh=mesh, in_specs=placed, out_specs=P("tile", "view", None), check_vma=False
    )
```
